32 devices in a mesh: tm: 8 (over z, core), pitch: 2 (over y), row: 2 (over x).
Axes of the slice: x: 2, y: 2, z: 4, core: 2. Of those that a mesh axis runs over, the one named last changes fastest.
Arguments:
- flow_state: float32 [2, 24, 5, 64, 256], P('row', 'tm', None, 'pitch'), may hold values from -6 to 6
- axial_jacobian: float32 [2, 5, 5], P('row'), may hold values from -2.5 to 2.5
- pitch_jacobian: float32 [2, 5, 5], P('row'), may hold values from -2.5 to 2.5
- inclination: float32 [2], P('row'), may hold values from 0.2 to 0.9
- interface_shift: int32 [2, 64], P('row', 'pitch'), may hold values from 0 to 23, as said below
- interface_rows: int32 [2, 64], P('row', 'pitch'), may hold values from 0 to 63, as said below
Outputs:
- new_state: float32 [2, 24, 5, 64, 256], P('row', 'tm', None, 'pitch')
The draws below stay inside these ranges and needn't reach their ends.
Inputs may be any that keep to these rules, and one draw needn't show every extreme that they name: interface_shift[r, j] = (s_r + floor(j * a_r / 64)) mod 24 for each row r, with whole numbers s_r in 0 to 23 and a_r in 1 to 23; some cell of row 0 has offset 0 and some cell of row 1 has offset 24 - 1. interface_rows[r, j] = (j + o_r) mod 64 for each row r, with a whole number o_r in 0 to 63.
All inputs are finite; a program needn't handle non-finite values.
Results may differ from the reference program's by a relative error of at most 0.00017.
Values sent between devices are 32-bit elements; how exact they have to be, the bound alone decides.
No kernel may reach another device: no remote copies, remote signals or barrier semaphores. Data moves between devices by JAX's collectives and lax.ppermute only.
A program may use at most 64 MiB of HBM per device.

```python
import jax
import jax.numpy as jnp
from jax import lax

NV = 5
SECTIONS = 4
NA = 256
NT = 24
NP = 64
N_ROW = 2


def draw_interface_shift(key, part):
    folded = jax.random.fold_in(key, 11)
    place_key, slope_key = jax.random.split(folded, 2)
    slopes = jax.random.randint(slope_key, (N_ROW, 1), 1, NT, dtype=jnp.int32)
    anchors = jax.random.randint(place_key, (N_ROW, 1), 0, NP, dtype=jnp.int32)
    targets = jnp.array([[0], [NT - 1]], dtype=jnp.int32)
    starts = (targets - anchors * slopes // NP) % NT
    places = jnp.arange(NP, dtype=jnp.int32)[None, :]
    return (starts + places * slopes // NP) % NT


def draw_interface_rows(key, part):
    folded = jax.random.fold_in(key, 23)
    offsets = jax.random.randint(folded, (N_ROW, 1), 0, NP, dtype=jnp.int32)
    places = jnp.arange(NP, dtype=jnp.int32)[None, :]
    return (places + offsets) % NP


def level_of(key, dims, cuts, low, largest):
    def one(position, blocks):
        draws = jax.random.uniform(jax.random.fold_in(jax.random.fold_in(key, 6), position), (blocks,), jnp.float32, low / len(cuts), largest / len(cuts))
        return jnp.repeat(jnp.exp(draws), dims[position] // blocks).reshape((-1,) + (1,) * (len(dims) - position - 1))

    loudness = one(*cuts[0])
    for cut in cuts[1:]:
        loudness = loudness * one(*cut)
    return loudness


def centred(key, extent, scale, most, shards=(), kind=jnp.bfloat16):
    gain = level_of(key, extent, shards, -0.22, 0.18) if shards else 1.0
    values = jax.random.normal(key, extent, jnp.float32) * scale * gain
    return jnp.minimum(jnp.maximum(values, -most), most).astype(kind)


def setup_inputs(seed: int = 0) -> dict:
    seeds = jax.random.split(jax.random.key(seed), 7)
    flow_state = centred(seeds[0], (N_ROW, NT, NV, NP, NA), 1.0, 6.0, ((0, 2), (1, 8), (3, 2)), jnp.float32)
    axial_jacobian = centred(seeds[1], (N_ROW, NV, NV), NV ** -0.5, 2.5, ((0, 2),), jnp.float32)
    pitch_jacobian = centred(seeds[2], (N_ROW, NV, NV), NV ** -0.5, 2.5, ((0, 2),), jnp.float32)
    inclination = jnp.clip(0.2 + 0.7 * jax.random.uniform(seeds[3], (N_ROW,), jnp.float32) ** level_of(seeds[3], (N_ROW,), ((0, 2),), -0.2, 0.2), 0.2, 0.9)
    interface_shift = draw_interface_shift(jax.random.fold_in(seeds[6], 71), 0)
    interface_rows = draw_interface_rows(jax.random.fold_in(seeds[6], 71), 0)
    return {"flow_state": flow_state, "axial_jacobian": axial_jacobian, "pitch_jacobian": pitch_jacobian, "inclination": inclination, "interface_shift": interface_shift, "interface_rows": interface_rows}


damping = 1.0 / 16.0


def apply_matrix(matrix, values):
    return jnp.einsum("vw,twpa->tvpa", matrix, values, precision=lax.Precision.HIGHEST)


def fourth_difference(minus_two, minus_one, center, plus_one, plus_two):
    return minus_two - 4.0 * minus_one + 6.0 * center - 4.0 * plus_one + plus_two


def time_derivative(minus_two, minus_one, plus_one, plus_two):
    return (minus_two - 8.0 * minus_one + 8.0 * plus_one - plus_two) / 12.0


def central_difference(minus_one, plus_one):
    return 0.5 * (plus_one - minus_one)


def row_residual(center, time_sides, pitch_sides, axial_sides, axial_matrix, pitch_matrix, time_matrix):
    time_rate = time_derivative(time_sides[0], time_sides[1], time_sides[2], time_sides[3])
    pitch_rate = central_difference(pitch_sides[1], pitch_sides[2])
    axial_rate = central_difference(axial_sides[1], axial_sides[2])
    smoothing = fourth_difference(time_sides[0], time_sides[1], center, time_sides[2], time_sides[3])
    smoothing = smoothing + fourth_difference(pitch_sides[0], pitch_sides[1], center, pitch_sides[2], pitch_sides[3])
    smoothing = smoothing + fourth_difference(axial_sides[0], axial_sides[1], center, axial_sides[2], axial_sides[3])
    total = apply_matrix(time_matrix, time_rate) + apply_matrix(axial_matrix, axial_rate)
    total = total + apply_matrix(pitch_matrix, pitch_rate)
    return total + damping * smoothing


def axial_neighbours(center, left_cells, right_cells):
    return (jnp.concatenate([left_cells, center[..., :-2]], axis=-1),
            jnp.concatenate([left_cells[..., 1:], center[..., :-1]], axis=-1),
            jnp.concatenate([center[..., 1:], right_cells[..., :1]], axis=-1),
            jnp.concatenate([center[..., 2:], right_cells], axis=-1))


def ghost_cells(source_strip, shifts, rows_map):
    levels = source_strip.shape[0]
    level_index = (jnp.arange(levels, dtype=jnp.int32)[:, None] + shifts.astype(jnp.int32)[None, :]) % levels
    picked = source_strip[level_index, :, rows_map.astype(jnp.int32)[None, :], :]
    return jnp.transpose(picked, (0, 2, 1, 3))


def full_residual(fields, axial_jacobian, pitch_jacobian, inclination, interface_shift, interface_rows):
    strips = (fields[0][..., -2:], fields[1][..., :2])
    outputs = []
    for row_number in range(2):
        center = fields[row_number]
        ghosts = ghost_cells(strips[1 - row_number], interface_shift[row_number], interface_rows[row_number])
        zero_cells = jnp.zeros_like(ghosts)
        if row_number == 0:
            axial_sides = axial_neighbours(center, zero_cells, ghosts)
        else:
            axial_sides = axial_neighbours(center, ghosts, zero_cells)
        time_sides = (jnp.roll(center, 2, 0), jnp.roll(center, 1, 0), jnp.roll(center, -1, 0), jnp.roll(center, -2, 0))
        pitch_sides = (jnp.roll(center, 2, 2), jnp.roll(center, 1, 2), jnp.roll(center, -1, 2), jnp.roll(center, -2, 2))
        identity = jnp.eye(center.shape[1], dtype=pitch_jacobian.dtype)
        time_matrix = identity - inclination[row_number] * pitch_jacobian[row_number]
        outputs.append(row_residual(center, time_sides, pitch_sides, axial_sides,
                                    axial_jacobian[row_number], pitch_jacobian[row_number], time_matrix))
    return jnp.stack(outputs)


def reference(flow_state, axial_jacobian, pitch_jacobian, inclination, interface_shift, interface_rows):
    current = flow_state
    for section_number in range(SECTIONS):
        factor = 1.0 / (SECTIONS - section_number)
        current = flow_state - factor * full_residual(current, axial_jacobian, pitch_jacobian, inclination,
                                                      interface_shift, interface_rows)
    return current
```

```python
import functools

import jax
import jax.numpy as jnp
from jax import lax
from jax.experimental import pallas as pl
from jax.experimental.pallas import tpu as pltpu
from jax.sharding import PartitionSpec as P

SECTIONS = 4
DAMPING = 1.0 / 16.0
LANES = 128
SUB = 8
WIDTH = 8
PATCHED = 4

VM = pl.BlockSpec(memory_space=pltpu.VMEM)
SM = pl.BlockSpec(memory_space=pltpu.SMEM)


def params(mib):
    return pltpu.CompilerParams(vmem_limit_bytes=mib << 20)


def ring(count, step):
    return [(i, (i + step) % count) for i in range(count)]


def f32(*shape):
    return jax.ShapeDtypeStruct(shape, jnp.float32)


def send_pack_kernel(x_ref, fwd_ref, bwd_ref, edge_ref):
    levels, variables, rows, axial = x_ref.shape
    fwd_ref[...] = x_ref[levels - 2 :]
    bwd_ref[...] = x_ref[:2]
    for t in range(levels):
        for v in range(variables):
            for h in range(axial // LANES):
                at = slice(h * LANES, (h + 1) * LANES)
                edge_ref[t, v, 4 * h : 4 * h + 2] = x_ref[t, v, 0:2, at]
                edge_ref[t, v, 4 * h + 2 : 4 * h + 4] = x_ref[t, v, rows - 2 : rows, at]


def local_kernel(section, has_pad, *refs):
    coef, bwd, fwd, init, edge = refs[:5]
    pad = refs[5] if has_pad else None
    out = refs[-1]
    levels, variables, rows, axial = init.shape
    tiles, groups = axial // LANES, rows // SUB
    factor = 1.0 / (SECTIONS - section)
    lane = lax.broadcasted_iota(jnp.int32, (SUB, LANES), 1)
    sub = lax.broadcasted_iota(jnp.int32, (SUB, LANES), 0)

    def cell(t, v, g, h):
        ref, index = (bwd, t) if t < 2 else (fwd, t - (levels - 2))
        return ref[index, v, SUB * g : SUB * g + SUB, h * LANES : (h + 1) * LANES]

    for g in range(groups):
        for h in range(tiles):
            center = {}
            for t in range(levels):
                for v in range(variables):
                    center[t, v] = cell(t, v, g, h)
            for t in range(levels):
                rates = []
                smooth = []
                for v in range(variables):
                    c = center[t, v]
                    if g == 0:
                        above = pltpu.roll(edge[t, v], (4 - 4 * h) % SUB, 0)
                    else:
                        above = cell(t, v, g - 1, h)
                    if g == groups - 1:
                        below = pltpu.roll(edge[t, v], (SUB - 4 * h) % SUB, 0)
                    else:
                        below = cell(t, v, g + 1, h)
                    j_m1 = pltpu.roll(jnp.where(sub >= 7, above, c), 1, 0)
                    j_m2 = pltpu.roll(jnp.where(sub >= 6, above, c), 2, 0)
                    j_p1 = pltpu.roll(jnp.where(sub < 1, below, c), 7, 0)
                    j_p2 = pltpu.roll(jnp.where(sub < 2, below, c), 6, 0)
                    beyond = (
                        pad[t, v, SUB * g : SUB * g + SUB] if has_pad else jnp.zeros_like(c)
                    )
                    left = beyond if h == 0 else cell(t, v, g, h - 1)
                    right = beyond if h == tiles - 1 else cell(t, v, g, h + 1)
                    a_m1 = pltpu.roll(jnp.where(lane >= LANES - 1, left, c), 1, 1)
                    a_m2 = pltpu.roll(jnp.where(lane >= LANES - 2, left, c), 2, 1)
                    a_p1 = pltpu.roll(jnp.where(lane < 1, right, c), LANES - 1, 1)
                    a_p2 = pltpu.roll(jnp.where(lane < 2, right, c), LANES - 2, 1)
                    near = (j_m1 + j_p1) + (a_m1 + a_p1)
                    far = (j_m2 + j_p2) + (a_m2 + a_p2)
                    rate = None
                    for step, weight in ((-2, 1.0), (-1, -8.0), (1, 8.0), (2, -1.0)):
                        if 0 <= t + step < levels:
                            u = center[t + step, v]
                            if abs(step) == 1:
                                near = near + u
                                u = weight * u
                                rate = u if rate is None else rate + u
                            else:
                                far = far + u
                                if rate is None:
                                    rate = weight * u
                                else:
                                    rate = rate + u if weight > 0 else rate - u
                    smooth.append(18.0 * c - 4.0 * near + far)
                    rates.append((rate, a_p1 - a_m1, j_p1 - j_m1))
                for v in range(variables):
                    total = smooth[v] * (-factor * DAMPING)
                    for w in range(variables):
                        for m in range(3):
                            total = total + coef[(m * variables + v) * variables + w] * rates[w][m]
                    at = (t, v, slice(SUB * g, SUB * g + SUB), slice(h * LANES, (h + 1) * LANES))
                    out[at] = init[at] + total


def remote_kernel(section, patched, last, *refs):
    coef, place, part, low, high = refs[:5]
    patch = refs[5] if patched else None
    outs = refs[6:] if patched else refs[5:]
    levels, variables, rows, axial = part.shape
    tiles, groups = axial // LANES, rows // SUB
    factor = 1.0 / (SECTIONS - section)
    if patched:
        lane = lax.broadcasted_iota(jnp.int32, (SUB, LANES), 1)
        rotor = place[0] == 0
    for g in range(groups):
        for h in range(tiles):
            js = slice(SUB * g, SUB * g + SUB)
            at = slice(h * LANES, (h + 1) * LANES)

            def level(t, v):
                if t < 0:
                    return low[t + 2, v, js, at]
                return high[t - levels, v, js, at]

            for t in range(levels):
                rates = []
                smooth = []
                for v in range(variables):
                    rate = None
                    near = None
                    far = None
                    for step, weight in ((-2, 1.0), (-1, -8.0), (1, 8.0), (2, -1.0)):
                        if not 0 <= t + step < levels:
                            u = level(t + step, v)
                            if abs(step) == 1:
                                near = u if near is None else near + u
                            else:
                                far = u if far is None else far + u
                            u = u if weight == 1.0 else weight * u
                            rate = u if rate is None else rate + u
                    q = None
                    if near is not None:
                        q = -4.0 * near
                    if far is not None:
                        q = far if q is None else q + far
                    rates.append(rate)
                    smooth.append(q)
                for v in range(variables):
                    total = smooth[v] * (-factor * DAMPING)
                    for w in range(variables):
                        total = total + coef[v * variables + w] * rates[w]
                    new = part[t, v, js, at] + total
                    if patched:
                        if h == 0:
                            new = jnp.where((lane < PATCHED) & ~rotor, patch[t, v, js], new)
                        if h == tiles - 1:
                            new = jnp.where(
                                (lane >= LANES - PATCHED) & rotor, patch[t, v, js], new
                            )
                    if last:
                        outs[0][t, v, js, at] = new
                        continue
                    fwd, bwd, edge = outs
                    if t < 2:
                        bwd[t, v, js, at] = new
                    if t >= levels - 2:
                        fwd[t - (levels - 2), v, js, at] = new
                    if g == 0:
                        edge[t, v, 4 * h : 4 * h + 2] = new[0:2]
                    if g == groups - 1:
                        edge[t, v, 4 * h + 2 : 4 * h + 4] = new[6:8]


def interface_kernel(blocks, slabs, rows, levels, variables, *refs):
    place, gathered, patch, pad2, pad3, coef, w0, w1, w2, w3, strip = refs
    span = slabs * rows
    lanes = 2 * span
    lane = lax.broadcasted_iota(jnp.int32, (blocks, lanes), 1)
    second = lane >= span
    j = jnp.where(second, lane - span, lane)
    part = lax.broadcasted_iota(jnp.int32, (blocks, LANES), 1) // rows
    per_tile = LANES // rows

    def spread(pick, shift_of):
        whole = []
        for tile in range(lanes // LANES):
            total = None
            for n in range(per_tile):
                x, y = divmod(per_tile * tile + n, slabs)
                moved = pltpu.roll(pick(x, y), (rows * (n - shift_of)) % LANES, 1)
                total = moved if total is None else jnp.where(part == n, moved, total)
            whole.append(total)
        return whole

    for hi in range(WIDTH // per_tile):
        for v in range(variables):
            for d in range(levels):
                row = (hi * variables + v) * levels + d
                got = {
                    (x, y): gathered[x, y, pl.ds(row, blocks, stride=32), :]
                    for x in range(2)
                    for y in range(slabs)
                }
                for lo in range(per_tile):
                    whole = spread(lambda x, y: got[x, y], lo)
                    for tile, value in enumerate(whole):
                        at = slice(tile * LANES, (tile + 1) * LANES)
                        w0[hi * per_tile + lo + 2, v, d, :, at] = value

    count = 3 * variables * variables
    first_row = [gathered[x, 0, 31:32, :] for x in range(2)]
    for k in range(count):
        coef[k] = jnp.where(second, first_row[1][:, k : k + 1], first_row[0][:, k : k + 1])

    def small(slot):
        whole = spread(
            lambda x, y: jnp.broadcast_to(gathered[x, y, 30:31, :], (blocks, LANES)), slot
        )
        whole = whole[0] if len(whole) == 1 else jnp.concatenate(whole, axis=1)
        return whole.astype(jnp.int32)

    shift = small(0)
    offset = small(1) - j
    offset = jnp.where(offset < 0, offset + span, offset)
    coarse = shift // levels
    fine = shift - levels * coarse

    def ahead(x, s):
        if s > 0:
            inside = j < span - s
        else:
            inside = j >= -s
        other = s - span if s > 0 else s + span
        return jnp.where(
            inside, pltpu.roll(x, -s % lanes, 1), pltpu.roll(x, -other % lanes, 1)
        )

    def later(w, c, v, d):
        if d >= levels:
            return pltpu.roll(w[c, v, d - levels], blocks - 1, 0)
        if d < 0:
            return pltpu.roll(w[c, v, d + levels], 1, 0)
        return w[c, v, d]

    def fill_ghosts(w):
        for c in range(2):
            for v in range(variables):
                seen = []
                for d in range(levels):
                    value = pltpu.roll(w[2 + c, v, d], span, 1)
                    for bit in range((span - 1).bit_length()):
                        moved = ahead(value, 1 << bit)
                        value = jnp.where((offset >> bit) & 1 == 1, moved, value)
                    seen.append(value)
                for d in range(levels):
                    value = seen[d]
                    for f in range(1, levels):
                        if d + f < levels:
                            moved = seen[d + f]
                        else:
                            moved = pltpu.roll(seen[d + f - levels], blocks - 1, 0)
                        value = jnp.where(fine == f, moved, value)
                    for bit in range((blocks - 1).bit_length()):
                        moved = pltpu.roll(value, blocks - (1 << bit), 0)
                        value = jnp.where((coarse >> bit) & 1 == 1, moved, value)
                    w[1 - c, v, d] = value

    def advance(w, new, cells, section):
        factor = 1.0 / (SECTIONS - section)

        def one(c, carry):
            for d in range(levels):
                rates = []
                smooth = []
                for v in range(variables):
                    u = w[c, v, d]
                    m2, m1, p1, p2 = (later(w, c, v, d + s) for s in (-2, -1, 1, 2))
                    y2, y1, z1, z2 = (ahead(u, s) for s in (-2, -1, 1, 2))
                    l2, l1 = w[c - 2, v, d], w[c - 1, v, d]
                    r1, r2 = w[c + 1, v, d], w[c + 2, v, d]
                    near = (m1 + p1) + (y1 + z1) + (l1 + r1)
                    far = (m2 + p2) + (y2 + z2) + (l2 + r2)
                    smooth.append(18.0 * u - 4.0 * near + far)
                    rates.append(((m2 - p2) + 8.0 * (p1 - m1), r1 - l1, z1 - y1))
                for v in range(variables):
                    total = smooth[v] * DAMPING
                    for m in range(3):
                        for k in range(variables):
                            total = total + coef[(m * variables + v) * variables + k] * rates[k][m]
                    new[c, v, d] = w0[c, v, d] - factor * total
            return carry

        lax.fori_loop(2, 2 + cells, one, 0)

    fill_ghosts(w0)
    advance(w0, w1, WIDTH - 2, 0)
    fill_ghosts(w1)
    advance(w1, w2, WIDTH - 4, 1)
    fill_ghosts(w2)
    advance(w2, w3, WIDTH - 6, 2)
    fill_ghosts(w3)

    row, block, slab = place[0], place[1], place[2]
    rotor = row == 0
    start = row * span + slab * rows
    out_lane = lax.broadcasted_iota(jnp.int32, (rows, LANES), 1)
    patch_mask = (out_lane >= jnp.where(rotor, LANES - PATCHED, 0)) & (
        out_lane < jnp.where(rotor, LANES, PATCHED)
    )
    pad_mask = (out_lane >= jnp.where(rotor, 0, LANES - 2)) & (
        out_lane < jnp.where(rotor, 2, LANES)
    )
    strip[...] = jnp.zeros(strip.shape, jnp.float32)
    for d in range(levels):
        for v in range(variables):
            for q in range(PATCHED):
                c = jnp.where(rotor, PATCHED - 1 - q, q)
                strip[q : q + 1, :] = w2[c + 2, v, d, pl.ds(block, 1), :]
            for q in range(2):
                k = jnp.where(rotor, 1 - q, q)
                strip[4 + q : 5 + q, :] = w2[k, v, d, pl.ds(block, 1), :]
                strip[6 + q : 7 + q, :] = w3[k, v, d, pl.ds(block, 1), :]
            own = pltpu.roll(strip[...], lanes - start, 1)[:, :LANES]
            turned = jnp.transpose(own)[:rows, :]
            wide = jnp.concatenate(
                [turned, jnp.zeros((rows, LANES - SUB), jnp.float32)], axis=1
            )
            lane0 = jnp.where(rotor, LANES - PATCHED, 0)
            patch[d, v] = jnp.where(patch_mask, pltpu.roll(wide, lane0, 1), 0.0)
            lane0 = jnp.where(rotor, 0, LANES - 2)
            pad2[d, v] = jnp.where(
                pad_mask, pltpu.roll(wide, lax.rem(lane0 + LANES - 4, LANES), 1), 0.0
            )
            pad3[d, v] = jnp.where(
                pad_mask, pltpu.roll(wide, lax.rem(lane0 + LANES - 6, LANES), 1), 0.0
            )


def gather_by_bits(piece, axis, dim, base):
    count = lax.axis_size(axis)
    index = lax.axis_index(axis)
    bits = (count - 1).bit_length()
    for n, bit in enumerate(reversed(range(bits))):
        other = lax.ppermute(piece, axis, [(i, i ^ (1 << bit)) for i in range(count)])
        upper = (index >> bit) & 1 == 1
        at = dim + n
        piece = jnp.where(
            upper,
            jnp.stack([other, piece], axis=at),
            jnp.stack([piece, other], axis=at),
        )
    return piece


def shards(
    flow_state, axial_jacobian, pitch_jacobian, inclination, interface_shift, interface_rows
):
    x = flow_state[0]
    levels, variables, rows, axial = x.shape
    blocks = lax.axis_size("tm")
    slabs = lax.axis_size("pitch")
    row_number = lax.axis_index("row")
    rotor = row_number == 0
    place = jnp.stack([row_number, lax.axis_index("tm"), lax.axis_index("pitch")]).astype(jnp.int32)

    time_matrix = jnp.eye(variables, dtype=jnp.float32) - inclination[0] * pitch_jacobian[0]
    matrices = jnp.stack([time_matrix / 12.0, 0.5 * axial_jacobian[0], 0.5 * pitch_jacobian[0]])
    flat = matrices.reshape(-1)
    coefs = [flat * (-1.0 / (SECTIONS - k)) for k in range(SECTIONS)]

    cells = jnp.where(rotor, x[..., axial - WIDTH :][..., ::-1], x[..., :WIDTH])
    lo = LANES // rows
    cells = cells.reshape(levels, variables, rows, WIDTH // lo, lo)
    cells = jnp.transpose(cells, (3, 1, 0, 4, 2)).reshape(-1, LANES)
    signs = jnp.stack([jnp.float32(1.0), jnp.where(rotor, -1.0, 1.0), jnp.float32(1.0)])
    signed = (matrices * signs[:, None, None]).reshape(-1)
    tables = jnp.concatenate([interface_shift[0], interface_rows[0]]).astype(jnp.float32)
    piece = jnp.concatenate(
        [
            cells,
            jnp.pad(tables, (0, LANES - tables.shape[0]))[None],
            jnp.pad(signed, (0, LANES - signed.shape[0]))[None],
        ]
    )

    state = (levels, variables, rows, axial)
    two = f32(2, variables, rows, axial)
    edge_shape = f32(levels, variables, SUB, LANES)
    fwd, bwd, edge = pl.pallas_call(
        send_pack_kernel,
        out_shape=(two, two, edge_shape),
        in_specs=[VM],
        out_specs=(VM, VM, VM),
        compiler_params=params(8),
    )(x)

    def exchange(fwd, bwd, edge):
        low = lax.ppermute(fwd, "tm", ring(blocks, 1))
        high = lax.ppermute(bwd, "tm", ring(blocks, -1))
        if slabs == 2:
            side = lax.ppermute(edge, "pitch", ring(2, 1))
        else:
            parts = edge.reshape(levels, variables, 2, 2, 2, LANES)
            below = lax.ppermute(parts[:, :, :, 0], "pitch", ring(slabs, -1))
            above = lax.ppermute(parts[:, :, :, 1], "pitch", ring(slabs, 1))
            side = jnp.stack([below, above], axis=3).reshape(edge.shape)
        return low, high, side

    def gather():
        part = gather_by_bits(piece, "pitch", 0, 0)
        ybits = (slabs - 1).bit_length()
        part = gather_by_bits(part, "tm", ybits, 0)
        part = gather_by_bits(part, "row", 0, 0)
        return part.reshape(2, slabs, blocks * 32, LANES)

    span = slabs * rows
    w_shape = lambda n: pltpu.VMEM((n + 2, variables, levels, blocks, 2 * span), jnp.float32)
    strip_shape = f32(levels, variables, rows, LANES)
    patch, pad2, pad3 = pl.pallas_call(
        functools.partial(interface_kernel, blocks, slabs, rows, levels, variables),
        out_shape=(strip_shape,) * 3,
        in_specs=[SM, VM],
        out_specs=(VM,) * 3,
        scratch_shapes=[
            pltpu.VMEM((3 * variables * variables, blocks, 2 * span), jnp.float32),
            w_shape(WIDTH),
            w_shape(WIDTH - 2),
            w_shape(WIDTH - 4),
            w_shape(WIDTH - 6),
            pltpu.VMEM((SUB, 2 * span), jnp.float32),
        ],
        compiler_params=params(8 if blocks * span <= 512 else 40),
    )(place, gather())

    for k in range(SECTIONS):
        low, high, side = exchange(fwd, bwd, edge)
        has_pad = k >= 2
        pads = [pad2 if k == 2 else pad3] if has_pad else []
        part = pl.pallas_call(
            functools.partial(local_kernel, k, has_pad),
            out_shape=f32(*state),
            in_specs=[SM] + [VM] * (4 + len(pads)),
            out_specs=VM,
            compiler_params=params(8),
        )(coefs[k], bwd, fwd, x, side, *pads)
        last = k == SECTIONS - 1
        patched = k == 1
        result = pl.pallas_call(
            functools.partial(remote_kernel, k, patched, last),
            out_shape=f32(*state) if last else (two, two, edge_shape),
            in_specs=[SM, SM] + [VM] * (4 if patched else 3),
            out_specs=VM if last else (VM, VM, VM),
            compiler_params=params(8),
        )(coefs[k], place, part, low, high, *([patch] if patched else []))
        if not last:
            fwd, bwd, edge = result
    return result[None]


def solution(mesh):
    return jax.shard_map(
        shards,
        mesh=mesh,
        in_specs=(
            P("row", "tm", None, "pitch", None),
            P("row", None, None),
            P("row", None, None),
            P("row"),
            P("row", "pitch"),
            P("row", "pitch"),
        ),
        out_specs=P("row", "tm", None, "pitch", None),
        check_vma=False,
    )
```

```python
import functools

import jax
import jax.numpy as jnp
from jax import lax
from jax.experimental import pallas as pl
from jax.experimental.pallas import tpu as pltpu
from jax.sharding import PartitionSpec as P


SECTIONS = 4
DAMPING = 1.0 / 16.0
LANES = 128
SUB = 8
WIDTH = 12
PATCHED = 6
GROUP = 4

VM = pl.BlockSpec(memory_space=pltpu.VMEM)
SM = pl.BlockSpec(memory_space=pltpu.SMEM)


def params(mib):
    return pltpu.CompilerParams(vmem_limit_bytes=mib << 20)


def ring(count, step):
    return [(i, (i + step) % count) for i in range(count)]


def f32(*shape):
    return jax.ShapeDtypeStruct(shape, jnp.float32)


def levels_pack_kernel(x_ref, fwd_ref, bwd_ref):
    levels = x_ref.shape[0]
    fwd_ref[...] = x_ref[levels - 2 :]
    bwd_ref[...] = x_ref[:2]


def piece_rows(levels, variables):
    return -(-(WIDTH // GROUP * levels * variables) // SUB) * SUB


def edge_pack_kernel(place, x_ref, edge_ref, piece_ref):
    levels, variables, rows, axial = x_ref.shape
    rotor = place[0] == 0
    slot = place[3]
    part = lax.broadcasted_iota(jnp.int32, (1, LANES), 1) // rows
    count = piece_ref.shape[0]
    used = WIDTH // GROUP * levels * variables
    piece_ref[used:, :] = jnp.zeros((count - used, LANES), jnp.float32)
    for t in range(levels):
        for v in range(variables):
            for h in range(axial // LANES):
                at = slice(h * LANES, (h + 1) * LANES)
                tile = t * variables + v
                edge_ref[tile, 4 * h : 4 * h + 2] = x_ref[t, v, 0:2, at]
                edge_ref[tile, 4 * h + 2 : 4 * h + 4] = x_ref[t, v, rows - 2 : rows, at]
            tile = jnp.where(rotor, x_ref[t, v, :, axial - LANES :], x_ref[t, v, :, :LANES])
            tile = jnp.transpose(tile)
            tile = jnp.where(rotor, tile[LANES - 2 * SUB :], tile[: 2 * SUB])
            tile = jnp.concatenate([tile] * GROUP, axis=1)
            for hi in range(WIDTH // GROUP):
                total = None
                for lo in range(GROUP):
                    c = hi * GROUP + lo
                    near = jnp.where(
                        rotor, tile[2 * SUB - 1 - c : 2 * SUB - c], tile[c : c + 1]
                    )
                    if total is None:
                        total = near
                    else:
                        total = jnp.where(part == lax.rem(lo + slot, GROUP), near, total)
                row = (hi * variables + v) * levels + t
                piece_ref[row : row + 1, :] = total


def local_kernel(section, has_pad, *refs):
    coef, place, bwd, fwd, init, edge = refs[:6]
    pad = refs[6] if has_pad else None
    rotor = place[0] == 0
    out = refs[-1]
    levels, variables, rows, axial = init.shape
    tiles, groups = axial // LANES, rows // SUB
    factor = 1.0 / (SECTIONS - section)
    lane = lax.broadcasted_iota(jnp.int32, (SUB, LANES), 1)
    sub = lax.broadcasted_iota(jnp.int32, (SUB, LANES), 0)

    def cell(t, v, g, h):
        ref, index = (bwd, t) if t < 2 else (fwd, t - (levels - 2))
        return ref[index, v, SUB * g : SUB * g + SUB, h * LANES : (h + 1) * LANES]

    for g in range(groups):
        for h in range(tiles):
            center = {}
            for t in range(levels):
                for v in range(variables):
                    center[t, v] = cell(t, v, g, h)
            for t in range(levels):
                rates = []
                smooth = []
                for v in range(variables):
                    c = center[t, v]
                    if g == 0:
                        above = pltpu.roll(edge[t * variables + v], (4 - 4 * h) % SUB, 0)
                    else:
                        above = cell(t, v, g - 1, h)
                    if g == groups - 1:
                        below = pltpu.roll(edge[t * variables + v], (SUB - 4 * h) % SUB, 0)
                    else:
                        below = cell(t, v, g + 1, h)
                    j_m1 = pltpu.roll(jnp.where(sub >= 7, above, c), 1, 0)
                    j_m2 = pltpu.roll(jnp.where(sub >= 6, above, c), 2, 0)
                    j_p1 = pltpu.roll(jnp.where(sub < 1, below, c), 7, 0)
                    j_p2 = pltpu.roll(jnp.where(sub < 2, below, c), 6, 0)
                    zero = jnp.zeros_like(c)
                    beyond = pad[t, v, SUB * g : SUB * g + SUB] if has_pad else zero
                    if h > 0:
                        left = cell(t, v, g, h - 1)
                    else:
                        left = jnp.where(rotor, zero, beyond) if has_pad else zero
                    if h < tiles - 1:
                        right = cell(t, v, g, h + 1)
                    else:
                        right = jnp.where(rotor, beyond, zero) if has_pad else zero
                    a_m1 = pltpu.roll(jnp.where(lane >= LANES - 1, left, c), 1, 1)
                    a_m2 = pltpu.roll(jnp.where(lane >= LANES - 2, left, c), 2, 1)
                    a_p1 = pltpu.roll(jnp.where(lane < 1, right, c), LANES - 1, 1)
                    a_p2 = pltpu.roll(jnp.where(lane < 2, right, c), LANES - 2, 1)
                    near = (j_m1 + j_p1) + (a_m1 + a_p1)
                    far = (j_m2 + j_p2) + (a_m2 + a_p2)
                    rate = None
                    for step, weight in ((-2, 1.0), (-1, -8.0), (1, 8.0), (2, -1.0)):
                        if 0 <= t + step < levels:
                            u = center[t + step, v]
                            if abs(step) == 1:
                                near = near + u
                                u = weight * u
                                rate = u if rate is None else rate + u
                            else:
                                far = far + u
                                if rate is None:
                                    rate = weight * u
                                else:
                                    rate = rate + u if weight > 0 else rate - u
                    smooth.append(18.0 * c - 4.0 * near + far)
                    rates.append((rate, a_p1 - a_m1, j_p1 - j_m1))
                for v in range(variables):
                    total = smooth[v] * (-factor * DAMPING)
                    for w in range(variables):
                        for m in range(3):
                            total = total + coef[(m * variables + v) * variables + w] * rates[w][m]
                    at = (t, v, slice(SUB * g, SUB * g + SUB), slice(h * LANES, (h + 1) * LANES))
                    out[at] = init[at] + total


def remote_kernel(section, patched, last, *refs):
    coef, place, part, low, high = refs[:5]
    patch = refs[5] if patched else None
    outs = refs[6:] if patched else refs[5:]
    levels, variables, rows, axial = part.shape
    tiles, groups = axial // LANES, rows // SUB
    factor = 1.0 / (SECTIONS - section)
    if patched:
        lane = lax.broadcasted_iota(jnp.int32, (SUB, LANES), 1)
        rotor = place[0] == 0
    for g in range(groups):
        for h in range(tiles):
            js = slice(SUB * g, SUB * g + SUB)
            at = slice(h * LANES, (h + 1) * LANES)

            def level(t, v):
                if t < 0:
                    return low[t + 2, v, js, at]
                return high[t - levels, v, js, at]

            for t in range(levels):
                rates = []
                smooth = []
                for v in range(variables):
                    rate = None
                    near = None
                    far = None
                    for step, weight in ((-2, 1.0), (-1, -8.0), (1, 8.0), (2, -1.0)):
                        if not 0 <= t + step < levels:
                            u = level(t + step, v)
                            if abs(step) == 1:
                                near = u if near is None else near + u
                            else:
                                far = u if far is None else far + u
                            u = u if weight == 1.0 else weight * u
                            rate = u if rate is None else rate + u
                    q = None
                    if near is not None:
                        q = -4.0 * near
                    if far is not None:
                        q = far if q is None else q + far
                    rates.append(rate)
                    smooth.append(q)
                for v in range(variables):
                    total = smooth[v] * (-factor * DAMPING)
                    for w in range(variables):
                        total = total + coef[v * variables + w] * rates[w]
                    new = part[t, v, js, at] + total
                    if patched:
                        if h == 0:
                            new = jnp.where((lane < PATCHED) & ~rotor, patch[t, v, js], new)
                        if h == tiles - 1:
                            new = jnp.where(
                                (lane >= LANES - PATCHED) & rotor, patch[t, v, js], new
                            )
                    if last:
                        outs[0][t, v, js, at] = new
                        continue
                    fwd, bwd, edge = outs
                    if t < 2:
                        bwd[t, v, js, at] = new
                    if t >= levels - 2:
                        fwd[t - (levels - 2), v, js, at] = new
                    if g == 0:
                        edge[t * variables + v, 4 * h : 4 * h + 2] = new[0:2]
                    if g == groups - 1:
                        edge[t * variables + v, 4 * h + 2 : 4 * h + 4] = new[6:8]


def unpack_interface(blocks, slabs, rows, levels, variables, part, refs):
    _, gathered, tables, w0, _, coef, shift_ref = refs
    span = slabs * rows
    lanes = 2 * span
    count = piece_rows(levels, variables)

    for hi in range(WIDTH // GROUP):
        for v in range(variables):
            for d in range(levels):
                row = (hi * variables + v) * levels + d
                for tile in range(lanes // LANES):
                    got = []
                    for n in range(GROUP):
                        x, y = divmod(GROUP * tile + n, slabs)
                        got.append(gathered[x, y, pl.ds(row, blocks, stride=count), :])
                    for lo in range(GROUP):
                        total = got[0]
                        for n in range(1, GROUP):
                            total = jnp.where(part == (lo + n) % GROUP, got[n], total)
                        if lo:
                            total = pltpu.roll(total, LANES - rows * lo, 1)
                        at = slice(tile * LANES, (tile + 1) * LANES)
                        w0[hi * GROUP + lo + 2, v, d, :, at] = total

    entries = 3 * variables * variables
    sides = []
    for x in range(2):
        turned = jnp.transpose(tables[x, 0])[:, 1:2]
        sides.append(jnp.broadcast_to(turned, (LANES, LANES)))
    lower = lax.broadcasted_iota(jnp.int32, (LANES, LANES), 1) >= span
    for tile in range(lanes // LANES):
        at = slice(tile * LANES, (tile + 1) * LANES)
        if lanes == LANES:
            both = jnp.where(lower, sides[1], sides[0])
        else:
            both = sides[(tile * LANES) // span]
        for k in range(entries):
            coef[k, :, at] = jnp.broadcast_to(both[k : k + 1], (blocks, LANES))

    for tile in range(lanes // LANES):
        total = None
        for n in range(GROUP):
            x, y = divmod(GROUP * tile + n, slabs)
            table = tables[x, y, 0:1, :]
            moved = jnp.broadcast_to(pltpu.roll(table, rows * n, 1) if n else table, (blocks, LANES))
            total = moved if total is None else jnp.where(part == n, moved, total)
        shift_ref[:, tile * LANES : (tile + 1) * LANES] = total


def interface_kernel(half, blocks, slabs, rows, levels, variables, *refs):
    if half == 0:
        offsets, _, _, w0, w1, coef, shift_ref = refs
    else:
        place, offsets, w0, w1, coef, shift_ref, strips, w2, w3, strip = refs
    span = slabs * rows
    lanes = 2 * span
    lane = lax.broadcasted_iota(jnp.int32, (blocks, lanes), 1)
    second = lane >= span
    j = jnp.where(second, lane - span, lane)
    part = lax.broadcasted_iota(jnp.int32, (blocks, LANES), 1) // rows
    if half == 0:
        unpack_interface(blocks, slabs, rows, levels, variables, part, refs)
    shift = shift_ref[...].astype(jnp.int32)
    coarse = shift // levels
    fine = shift - levels * coarse

    def neighbours(u):
        around = pltpu.roll(u, span, 1)
        out = []
        for s in (-2, -1, 1, 2):
            wraps = (j >= span + s) if s < 0 else (j < s)
            out.append(pltpu.roll(jnp.where(wraps, around, u), -s % lanes, 1))
        return out

    def later(w, c, v, d):
        if d >= levels:
            return pltpu.roll(w[c, v, d - levels], blocks - 1, 0)
        if d < 0:
            return pltpu.roll(w[c, v, d + levels], 1, 0)
        return w[c, v, d]

    turn = [lanes - offsets[r] for r in range(2)]

    def fill_ghosts(w):
        for c in range(2):
            for v in range(variables):
                seen = []
                for d in range(levels):
                    u = w[2 + c, v, d]
                    around = pltpu.roll(u, span, 1)
                    rotors = pltpu.roll(jnp.where(second, around, u), turn[1], 1)
                    stators = pltpu.roll(jnp.where(second, u, around), turn[0], 1)
                    seen.append(jnp.where(second, rotors, stators))
                wrapped = [pltpu.roll(seen[d], blocks - 1, 0) for d in range(levels - 1)]
                for d in range(levels):
                    value = seen[d]
                    for f in range(1, levels):
                        moved = seen[d + f] if d + f < levels else wrapped[d + f - levels]
                        value = jnp.where(fine == f, moved, value)
                    for bit in range((blocks - 1).bit_length()):
                        moved = pltpu.roll(value, blocks - (1 << bit), 0)
                        value = jnp.where((coarse >> bit) & 1 == 1, moved, value)
                    w[1 - c, v, d] = value

    def advance(w, new, cells, section):
        factor = 1.0 / (SECTIONS - section)

        def one(c, carry):
            for d in range(levels):
                rates = []
                smooth = []
                for v in range(variables):
                    u = w[c, v, d]
                    m2, m1, p1, p2 = (later(w, c, v, d + s) for s in (-2, -1, 1, 2))
                    y2, y1, z1, z2 = neighbours(u)
                    l2, l1 = w[c - 2, v, d], w[c - 1, v, d]
                    r1, r2 = w[c + 1, v, d], w[c + 2, v, d]
                    near = (m1 + p1) + (y1 + z1) + (l1 + r1)
                    far = (m2 + p2) + (y2 + z2) + (l2 + r2)
                    smooth.append(18.0 * u - 4.0 * near + far)
                    rates.append(((m2 - p2) + 8.0 * (p1 - m1), r1 - l1, z1 - y1))
                for v in range(variables):
                    total = smooth[v] * DAMPING
                    for m in range(3):
                        for k in range(variables):
                            total = total + coef[(m * variables + v) * variables + k] * rates[k][m]
                    new[c, v, d] = w0[c, v, d] - factor * total
            return carry

        lax.fori_loop(2, 2 + cells, one, 0)

    if half == 0:
        fill_ghosts(w0)
        advance(w0, w1, WIDTH - 2, 0)
        fill_ghosts(w1)
        return
    advance(w1, w2, WIDTH - 4, 1)
    fill_ghosts(w2)
    advance(w2, w3, WIDTH - 6, 2)
    fill_ghosts(w3)

    row, block, slab = place[0], place[1], place[2]
    rotor = row == 0
    start = row * span + slab * rows
    first_lane = jnp.where(rotor, LANES - PATCHED, LANES - 2)
    for d in range(levels):
        for v in range(variables):
            for q in range(SUB):
                c = jnp.where(rotor, SUB - 1 - q, q)
                strip[q : q + 1, :] = w3[c, v, d, pl.ds(block, 1), :]
            own = pltpu.roll(strip[...], lanes - start, 1)[:, :LANES]
            turned = jnp.transpose(own)[:rows, :]
            wide = jnp.concatenate(
                [turned, jnp.zeros((rows, LANES - SUB), jnp.float32)], axis=1
            )
            strips[d, v] = pltpu.roll(wide, first_lane, 1)


def exchange_bit(piece, axis, bit, at):
    count = lax.axis_size(axis)
    other = lax.ppermute(piece, axis, [(i, i ^ (1 << bit)) for i in range(count)])
    return join(piece, other, axis, bit, at)


def join(piece, other, axis, bit, at):
    upper = (lax.axis_index(axis) >> bit) & 1 == 1
    return jnp.where(
        upper, jnp.stack([other, piece], axis=at), jnp.stack([piece, other], axis=at)
    )


def shards(
    flow_state, axial_jacobian, pitch_jacobian, inclination, interface_shift, interface_rows
):
    x = flow_state[0]
    levels, variables, rows, axial = x.shape
    blocks = lax.axis_size("tm")
    slabs = lax.axis_size("pitch")
    row_number = lax.axis_index("row")
    slab = lax.axis_index("pitch")
    rotor = row_number == 0
    slot = (row_number * slabs + slab) % GROUP
    place = jnp.stack([row_number, lax.axis_index("tm"), slab, slot]).astype(jnp.int32)

    time_matrix = jnp.eye(variables, dtype=jnp.float32) - inclination[0] * pitch_jacobian[0]
    matrices = jnp.stack([time_matrix / 12.0, 0.5 * axial_jacobian[0], 0.5 * pitch_jacobian[0]])
    flat = matrices.reshape(-1)
    coefs = [flat * (-1.0 / (SECTIONS - k)) for k in range(SECTIONS)]
    signs = jnp.stack([jnp.float32(1.0), jnp.where(rotor, -1.0, 1.0), jnp.float32(1.0)])
    signed = (matrices * signs[:, None, None]).reshape(-1)
    tables = jnp.concatenate([interface_shift[0], interface_rows[0]]).astype(jnp.float32)
    tables = jnp.pad(
        jnp.stack(
            [
                jnp.pad(tables, (0, LANES - tables.shape[0])),
                jnp.pad(signed, (0, LANES - signed.shape[0])),
            ]
        ),
        ((0, SUB - 2), (0, 0)),
    )

    two = f32(2, variables, rows, axial)
    edge_shape = f32(levels * variables, SUB, LANES)
    piece_size = piece_rows(levels, variables)

    fwd, bwd = pl.pallas_call(
        levels_pack_kernel,
        out_shape=(two, two),
        in_specs=[VM],
        out_specs=(VM, VM),
        compiler_params=params(8),
    )(x)
    edge, piece = pl.pallas_call(
        edge_pack_kernel,
        out_shape=(edge_shape, f32(piece_size, LANES)),
        in_specs=[SM, VM],
        out_specs=(VM, VM),
        compiler_params=params(8),
    )(place, x)

    def pitch_sides(edge):
        if slabs == 2:
            return lax.ppermute(edge, "pitch", ring(2, 1))
        parts = edge.reshape(levels * variables, 2, 2, 2, LANES)
        below = lax.ppermute(parts[:, :, 0], "pitch", ring(slabs, -1))
        above = lax.ppermute(parts[:, :, 1], "pitch", ring(slabs, 1))
        return jnp.stack([below, above], axis=2).reshape(edge.shape)

    span = slabs * rows
    lanes = 2 * span
    entries = 3 * variables * variables
    w_shape = lambda n: (n + 2, variables, levels, blocks, lanes)
    limit = params(10 if blocks * span <= 512 else 60)
    tiles = levels * variables

    tbits = (blocks - 1).bit_length()
    ybits = (slabs - 1).bit_length()
    part = piece
    for n in range(tbits - 1):
        part = exchange_bit(part, "tm", tbits - 1 - n, n)
    bundle = jnp.concatenate([part.reshape(-1, SUB, LANES), tables[None]])

    for k in range(SECTIONS):
        low = lax.ppermute(fwd, "tm", ring(blocks, 1))
        high = lax.ppermute(bwd, "tm", ring(blocks, -1))
        if k == 0:
            if slabs == 2:
                side = pitch_sides(jnp.concatenate([edge, bundle]))
                bundle = join(bundle, side[tiles:], "pitch", 0, 0)
            else:
                side = pitch_sides(edge)
                for n in range(ybits):
                    bundle = exchange_bit(bundle, "pitch", ybits - 1 - n, n)
            bundle = exchange_bit(bundle, "row", 0, 0)
            bundle = bundle.reshape((2, slabs) + bundle.shape[-3:])
            tables = bundle[:, :, -1]
            part = bundle[:, :, :-1].reshape(2, slabs, blocks // 2, piece_size, LANES)
            part = exchange_bit(part, "tm", 0, 3)
            part = part.reshape(2, slabs, blocks * piece_size, LANES)
            offsets = tables[:, 0, 0, rows].astype(jnp.int32)
            w0, w1, coef, shift = pl.pallas_call(
                functools.partial(interface_kernel, 0, blocks, slabs, rows, levels, variables),
                out_shape=(
                    f32(*w_shape(WIDTH)),
                    f32(*w_shape(WIDTH - 2)),
                    f32(entries, blocks, lanes),
                    f32(blocks, lanes),
                ),
                in_specs=[SM, VM, VM],
                out_specs=(VM,) * 4,
                compiler_params=limit,
            )(offsets, part, tables)
            strips = pl.pallas_call(
                functools.partial(interface_kernel, 1, blocks, slabs, rows, levels, variables),
                out_shape=f32(levels, variables, rows, LANES),
                in_specs=[SM, SM] + [VM] * 4,
                out_specs=VM,
                scratch_shapes=[
                    pltpu.VMEM(w_shape(WIDTH - 4), jnp.float32),
                    pltpu.VMEM(w_shape(WIDTH - 6), jnp.float32),
                    pltpu.VMEM((SUB, lanes), jnp.float32),
                ],
                compiler_params=limit,
            )(place, offsets, w0, w1, coef, shift)
        else:
            side = pitch_sides(edge)
        last = k == SECTIONS - 1
        patched = k == SECTIONS - 2
        extra = [strips] if last else []
        inner = pl.pallas_call(
            functools.partial(local_kernel, k, last),
            out_shape=f32(levels, variables, rows, axial),
            in_specs=[SM, SM] + [VM] * (4 + len(extra)),
            out_specs=VM,
            compiler_params=params(8),
        )(coefs[k], place, bwd, fwd, x, side, *extra)
        extra = [strips] if patched else []
        result = pl.pallas_call(
            functools.partial(remote_kernel, k, patched, last),
            out_shape=f32(levels, variables, rows, axial) if last else (two, two, edge_shape),
            in_specs=[SM, SM] + [VM] * (3 + len(extra)),
            out_specs=VM if last else (VM, VM, VM),
            compiler_params=params(8),
        )(coefs[k], place, inner, low, high, *extra)
        if not last:
            fwd, bwd, edge = result
    return result[None]


def solution(mesh):
    return jax.shard_map(
        shards,
        mesh=mesh,
        in_specs=(
            P("row", "tm", None, "pitch", None),
            P("row", None, None),
            P("row", None, None),
            P("row"),
            P("row", "pitch"),
            P("row", "pitch"),
        ),
        out_specs=P("row", "tm", None, "pitch", None),
        check_vma=False,
    )
```

```python
import functools

import jax
import jax.numpy as jnp
from jax import lax
from jax.experimental import pallas as pl
from jax.experimental.pallas import tpu as pltpu
from jax.sharding import PartitionSpec as P


SECTIONS = 4
DAMPING = 1.0 / 16.0
LANES = 128
SUB = 8
WIDTH = 12
PATCHED = 6
GROUP = 4

VM = pl.BlockSpec(memory_space=pltpu.VMEM)
SM = pl.BlockSpec(memory_space=pltpu.SMEM)


def params(mib):
    return pltpu.CompilerParams(vmem_limit_bytes=mib << 20)


def ring(count, step):
    return [(i, (i + step) % count) for i in range(count)]


def f32(*shape):
    return jax.ShapeDtypeStruct(shape, jnp.float32)


def levels_pack_kernel(x_ref, fwd_ref, bwd_ref):
    levels = x_ref.shape[0]
    fwd_ref[...] = x_ref[levels - 2 :]
    bwd_ref[...] = x_ref[:2]


def piece_rows(levels, variables):
    return -(-(WIDTH // GROUP * levels * variables) // SUB) * SUB


def edge_pack_kernel(place, x_ref, edge_ref, piece_ref):
    levels, variables, rows, axial = x_ref.shape
    rotor = place[0] == 0
    slot = place[3]
    part = lax.broadcasted_iota(jnp.int32, (1, LANES), 1) // rows
    count = piece_ref.shape[0]
    used = WIDTH // GROUP * levels * variables
    piece_ref[used:, :] = jnp.zeros((count - used, LANES), jnp.float32)
    for t in range(levels):
        for v in range(variables):
            for h in range(axial // LANES):
                at = slice(h * LANES, (h + 1) * LANES)
                tile = t * variables + v
                edge_ref[tile, 4 * h : 4 * h + 2] = x_ref[t, v, 0:2, at]
                edge_ref[tile, 4 * h + 2 : 4 * h + 4] = x_ref[t, v, rows - 2 : rows, at]
            tile = jnp.where(rotor, x_ref[t, v, :, axial - LANES :], x_ref[t, v, :, :LANES])
            tile = jnp.transpose(tile)
            tile = jnp.where(rotor, tile[LANES - 2 * SUB :], tile[: 2 * SUB])
            tile = jnp.concatenate([tile] * GROUP, axis=1)
            for hi in range(WIDTH // GROUP):
                total = None
                for lo in range(GROUP):
                    c = hi * GROUP + lo
                    near = jnp.where(
                        rotor, tile[2 * SUB - 1 - c : 2 * SUB - c], tile[c : c + 1]
                    )
                    if total is None:
                        total = near
                    else:
                        total = jnp.where(part == lax.rem(lo + slot, GROUP), near, total)
                row = (hi * variables + v) * levels + t
                piece_ref[row : row + 1, :] = total


def tables_kernel(place, *refs):
    tables, sems = refs[5], refs[11]
    copies = [pltpu.make_async_copy(refs[n], refs[6 + n], sems.at[n]) for n in range(5)]
    for copy in copies:
        copy.start()
    axial_ref, pitch_ref, lean_ref, shift_ref, cells_ref = refs[6:11]
    rotor = place[0] == 0
    variables, rows = axial_ref.shape[0], shift_ref.shape[1]
    for copy in copies:
        copy.wait()
    tables[0] = jnp.zeros((SUB, LANES), jnp.float32)
    tables[0, 0:1, :rows] = shift_ref[...].astype(jnp.float32)
    tables[0, 0:1, rows : 2 * rows] = cells_ref[...].astype(jnp.float32)
    lane = lax.broadcasted_iota(jnp.int32, (1, LANES), 1)
    entries = jnp.zeros((1, LANES), jnp.float32)
    side = jnp.where(rotor, -0.5, 0.5)
    for v in range(variables):
        for w in range(variables):
            turn = (1.0 if v == w else 0.0) - lean_ref[0] * pitch_ref[v, 0, w]
            values = (turn * (1.0 / 12.0), side * axial_ref[v, 0, w], 0.5 * pitch_ref[v, 0, w])
            for m, value in enumerate(values):
                entries = jnp.where(lane == (m * variables + v) * variables + w, value, entries)
    tables[0, 1:2, :] = entries


def local_kernel(section, has_pad, *refs):
    coef, place, bwd, fwd, init, edge = refs[:6]
    pad = refs[6] if has_pad else None
    rotor = place[0] == 0
    out = refs[-1]
    levels, variables, rows, axial = init.shape
    tiles, groups = axial // LANES, rows // SUB
    factor = 1.0 / (SECTIONS - section)
    lane = lax.broadcasted_iota(jnp.int32, (SUB, LANES), 1)
    sub = lax.broadcasted_iota(jnp.int32, (SUB, LANES), 0)

    def cell(t, v, g, h):
        ref, index = (bwd, t) if t < 2 else (fwd, t - (levels - 2))
        return ref[index, v, SUB * g : SUB * g + SUB, h * LANES : (h + 1) * LANES]

    for g in range(groups):
        for h in range(tiles):
            center = {}
            for t in range(levels):
                for v in range(variables):
                    center[t, v] = cell(t, v, g, h)
            for t in range(levels):
                rates = []
                smooth = []
                for v in range(variables):
                    c = center[t, v]
                    if g == 0:
                        above = pltpu.roll(edge[t * variables + v], (4 - 4 * h) % SUB, 0)
                    else:
                        above = cell(t, v, g - 1, h)
                    if g == groups - 1:
                        below = pltpu.roll(edge[t * variables + v], (SUB - 4 * h) % SUB, 0)
                    else:
                        below = cell(t, v, g + 1, h)
                    j_m1 = pltpu.roll(jnp.where(sub >= 7, above, c), 1, 0)
                    j_m2 = pltpu.roll(jnp.where(sub >= 6, above, c), 2, 0)
                    j_p1 = pltpu.roll(jnp.where(sub < 1, below, c), 7, 0)
                    j_p2 = pltpu.roll(jnp.where(sub < 2, below, c), 6, 0)
                    zero = jnp.zeros_like(c)
                    beyond = pad[t, v, SUB * g : SUB * g + SUB] if has_pad else zero
                    if h > 0:
                        left = cell(t, v, g, h - 1)
                    else:
                        left = jnp.where(rotor, zero, beyond) if has_pad else zero
                    if h < tiles - 1:
                        right = cell(t, v, g, h + 1)
                    else:
                        right = jnp.where(rotor, beyond, zero) if has_pad else zero
                    a_m1 = pltpu.roll(jnp.where(lane >= LANES - 1, left, c), 1, 1)
                    a_m2 = pltpu.roll(jnp.where(lane >= LANES - 2, left, c), 2, 1)
                    a_p1 = pltpu.roll(jnp.where(lane < 1, right, c), LANES - 1, 1)
                    a_p2 = pltpu.roll(jnp.where(lane < 2, right, c), LANES - 2, 1)
                    near = (j_m1 + j_p1) + (a_m1 + a_p1)
                    far = (j_m2 + j_p2) + (a_m2 + a_p2)
                    rate = None
                    for step, weight in ((-2, 1.0), (-1, -8.0), (1, 8.0), (2, -1.0)):
                        if 0 <= t + step < levels:
                            u = center[t + step, v]
                            if abs(step) == 1:
                                near = near + u
                                u = weight * u
                                rate = u if rate is None else rate + u
                            else:
                                far = far + u
                                if rate is None:
                                    rate = weight * u
                                else:
                                    rate = rate + u if weight > 0 else rate - u
                    smooth.append(18.0 * c - 4.0 * near + far)
                    rates.append((rate, a_p1 - a_m1, j_p1 - j_m1))
                for v in range(variables):
                    total = smooth[v] * DAMPING
                    for w in range(variables):
                        for m in range(3):
                            total = total + coef[(m * variables + v) * variables + w] * rates[w][m]
                    at = (t, v, slice(SUB * g, SUB * g + SUB), slice(h * LANES, (h + 1) * LANES))
                    out[at] = init[at] - factor * total


def remote_kernel(section, patched, last, *refs):
    coef, place, part, low, high = refs[:5]
    patch = refs[5] if patched else None
    outs = refs[6:] if patched else refs[5:]
    levels, variables, rows, axial = part.shape
    if last:
        result, built, sems = outs
        outs = (built,)
    tiles, groups = axial // LANES, rows // SUB
    factor = 1.0 / (SECTIONS - section)
    if patched:
        lane = lax.broadcasted_iota(jnp.int32, (SUB, LANES), 1)
        rotor = place[0] == 0

    def block(g, h, wanted):
        js = slice(SUB * g, SUB * g + SUB)
        at = slice(h * LANES, (h + 1) * LANES)

        def level(t, v):
            if t < 0:
                return low[t + 2, v, js, at]
            return high[t - levels, v, js, at]

        for t in wanted:
            rates = []
            smooth = []
            for v in range(variables):
                rate = None
                near = None
                far = None
                for step, weight in ((-2, 1.0), (-1, -8.0), (1, 8.0), (2, -1.0)):
                    if not 0 <= t + step < levels:
                        u = level(t + step, v)
                        if abs(step) == 1:
                            near = u if near is None else near + u
                        else:
                            far = u if far is None else far + u
                        u = u if weight == 1.0 else weight * u
                        rate = u if rate is None else rate + u
                q = None
                if near is not None:
                    q = -4.0 * near
                if far is not None:
                    q = far if q is None else q + far
                rates.append(rate)
                smooth.append(q)
            for v in range(variables):
                total = smooth[v] * DAMPING
                for w in range(variables):
                    total = total + coef[v * variables + w] * rates[w]
                new = part[t, v, js, at] - factor * total
                if patched:
                    if h == 0:
                        new = jnp.where((lane < PATCHED) & ~rotor, patch[t, v, js], new)
                    if h == tiles - 1:
                        new = jnp.where(
                            (lane >= LANES - PATCHED) & rotor, patch[t, v, js], new
                        )
                if last:
                    outs[0][t, v, js, at] = new
                    continue
                fwd, bwd, edge = outs
                if t < 2:
                    bwd[t, v, js, at] = new
                if t >= levels - 2:
                    fwd[t - (levels - 2), v, js, at] = new
                if g == 0:
                    edge[t * variables + v, 4 * h : 4 * h + 2] = new[0:2]
                if g == groups - 1:
                    edge[t * variables + v, 4 * h + 2 : 4 * h + 4] = new[6:8]

    if not last:
        for g in range(groups):
            for h in range(tiles):
                block(g, h, range(levels))
        return
    copies = []
    for t in range(levels):
        for g in range(groups):
            for h in range(tiles):
                block(g, h, (t,))
        copies.append(pltpu.make_async_copy(built.at[t], result.at[t], sems.at[t]))
        copies[-1].start()
    for copy in copies:
        copy.wait()


def unpack_interface(blocks, slabs, rows, levels, variables, part, refs):
    _, gathered, tables, w0, _, coef, shift_ref, _, _ = refs
    span = slabs * rows
    lanes = 2 * span
    count = piece_rows(levels, variables)

    for hi in range(WIDTH // GROUP):
        for v in range(variables):
            for d in range(levels):
                row = (hi * variables + v) * levels + d
                for tile in range(lanes // LANES):
                    got = []
                    for n in range(GROUP):
                        x, y = divmod(GROUP * tile + n, slabs)
                        got.append(gathered[x, y, pl.ds(row, blocks, stride=count), :])
                    for lo in range(GROUP):
                        total = got[0]
                        for n in range(1, GROUP):
                            total = jnp.where(part == (lo + n) % GROUP, got[n], total)
                        if lo:
                            total = pltpu.roll(total, LANES - rows * lo, 1)
                        at = slice(tile * LANES, (tile + 1) * LANES)
                        w0[hi * GROUP + lo + 2, v, d, :, at] = total

    sides = []
    for x in range(2):
        turned = jnp.transpose(tables[x, 0])[:, 1:2]
        sides.append(jnp.broadcast_to(turned, (LANES, LANES)))
    lower = lax.broadcasted_iota(jnp.int32, (LANES, LANES), 1) >= span
    for tile in range(lanes // LANES):
        at = slice(tile * LANES, (tile + 1) * LANES)
        if lanes == LANES:
            both = jnp.where(lower, sides[1], sides[0])
        else:
            both = sides[(tile * LANES) // span]
        coef[:, at] = both[: coef.shape[0]]

    for tile in range(lanes // LANES):
        total = None
        for n in range(GROUP):
            x, y = divmod(GROUP * tile + n, slabs)
            table = tables[x, y, 0:1, :]
            moved = jnp.broadcast_to(pltpu.roll(table, rows * n, 1) if n else table, (blocks, LANES))
            total = moved if total is None else jnp.where(part == n, moved, total)
        shift_ref[:, tile * LANES : (tile + 1) * LANES] = total


def interface_kernel(half, blocks, slabs, rows, levels, variables, *refs):
    if half == 0:
        offsets, _, _, w0, w1, coef, shift_ref, smooth_terms, rate_terms = refs
    else:
        place, offsets, w0, w1, coef, shift_ref, strips, w2, w3, strip, smooth_terms, rate_terms = refs
    span = slabs * rows
    lanes = 2 * span
    lane = lax.broadcasted_iota(jnp.int32, (blocks, lanes), 1)
    second = lane >= span
    part = lax.broadcasted_iota(jnp.int32, (blocks, LANES), 1) // rows
    if half == 0:
        unpack_interface(blocks, slabs, rows, levels, variables, part, refs)
    shift = shift_ref[...].astype(jnp.int32)
    coarse = shift // levels
    fine = shift - levels * coarse

    source = lax.broadcasted_iota(jnp.int32, (lanes, lanes), 0)
    target = lax.broadcasted_iota(jnp.int32, (lanes, lanes), 1)
    base = jnp.where(target >= span, span, 0)
    cell = target - base

    def picks(s):
        return (source == base + lax.rem(cell + (span + s), span)).astype(jnp.float32)

    one_away = picks(-1), picks(1)
    smoothing = (picks(-2) + picks(2)) - 4.0 * (one_away[0] + one_away[1])
    pitch_terms = jnp.concatenate([smoothing, one_away[1] - one_away[0]], axis=1)
    read = lax.rem(cell + jnp.where(target >= span, offsets[1], offsets[0]), span)
    remap = (source == (span - base) + read).astype(jnp.float32)

    def for_parts(matrix):
        return jnp.concatenate([matrix.astype(jnp.bfloat16)] * 3, axis=0)

    pitch_terms, remap = for_parts(pitch_terms), for_parts(remap)

    def product(u, matrix):
        high = u.astype(jnp.bfloat16)
        rest = u - high.astype(jnp.float32)
        middle = rest.astype(jnp.bfloat16)
        low = (rest - middle.astype(jnp.float32)).astype(jnp.bfloat16)
        parts = jnp.concatenate([high, middle, low], axis=1)
        return jnp.dot(parts, matrix, preferred_element_type=jnp.float32)

    pair_shape = (2, variables, levels, blocks, lanes)

    def flat(w, c):
        return w[c : c + 2].reshape(-1, lanes)

    def later(w, c, v, d):
        if d >= levels:
            return pltpu.roll(w[c, v, d - levels], blocks - 1, 0)
        if d < 0:
            return pltpu.roll(w[c, v, d + levels], 1, 0)
        return w[c, v, d]

    def fill_ghosts(w):
        moved_cells = product(flat(w, 2), remap).reshape(pair_shape)
        for c in range(2):
            for v in range(variables):
                seen = [moved_cells[c, v, d] for d in range(levels)]
                wrapped = [pltpu.roll(seen[d], blocks - 1, 0) for d in range(levels - 1)]
                for d in range(levels):
                    value = seen[d]
                    for f in range(1, levels):
                        moved = seen[d + f] if d + f < levels else wrapped[d + f - levels]
                        value = jnp.where(fine == f, moved, value)
                    for bit in range((blocks - 1).bit_length()):
                        moved = pltpu.roll(value, blocks - (1 << bit), 0)
                        value = jnp.where((coarse >> bit) & 1 == 1, moved, value)
                    w[1 - c, v, d] = value

    def across(w, cells):
        for c in range(0, cells, 2):
            terms = product(flat(w, c + 2), pitch_terms)
            smooth_terms[c : c + 2] = terms[:, :lanes].reshape(pair_shape)
            rate_terms[c : c + 2] = terms[:, lanes:].reshape(pair_shape)

    def advance(w, new, cells, section):
        factor = 1.0 / (SECTIONS - section)

        def one(c, carry):
            for d in range(levels):
                rates = []
                smooth = []
                for v in range(variables):
                    u = w[c, v, d]
                    m2, m1, p1, p2 = (later(w, c, v, d + s) for s in (-2, -1, 1, 2))
                    l2, l1 = w[c - 2, v, d], w[c - 1, v, d]
                    r1, r2 = w[c + 1, v, d], w[c + 2, v, d]
                    near = (m1 + p1) + (l1 + r1)
                    far = (m2 + p2) + (l2 + r2)
                    smooth.append((18.0 * u - 4.0 * near) + (far + smooth_terms[c - 2, v, d]))
                    rates.append(((m2 - p2) + 8.0 * (p1 - m1), r1 - l1, rate_terms[c - 2, v, d]))
                for v in range(variables):
                    total = smooth[v] * DAMPING
                    for m in range(3):
                        for k in range(variables):
                            at = (m * variables + v) * variables + k
                            total = total + coef[at : at + 1, :] * rates[k][m]
                    new[c, v, d] = w0[c, v, d] - factor * total
            return carry

        across(w, cells)
        lax.fori_loop(2, 2 + cells, one, 0)

    if half == 0:
        fill_ghosts(w0)
        advance(w0, w1, WIDTH - 2, 0)
        fill_ghosts(w1)
        return
    advance(w1, w2, WIDTH - 4, 1)
    fill_ghosts(w2)
    advance(w2, w3, WIDTH - 6, 2)
    fill_ghosts(w3)

    row, block, slab = place[0], place[1], place[2]
    rotor = row == 0
    start = row * span + slab * rows
    first_lane = jnp.where(rotor, LANES - PATCHED, LANES - 2)
    for d in range(levels):
        for v in range(variables):
            for q in range(SUB):
                c = jnp.where(rotor, SUB - 1 - q, q)
                strip[q : q + 1, :] = w3[c, v, d, pl.ds(block, 1), :]
            own = pltpu.roll(strip[...], lanes - start, 1)[:, :LANES]
            turned = jnp.transpose(own)[:rows, :]
            wide = jnp.concatenate(
                [turned, jnp.zeros((rows, LANES - SUB), jnp.float32)], axis=1
            )
            strips[d, v] = pltpu.roll(wide, first_lane, 1)


def exchange_bit(piece, axis, bit, at):
    count = lax.axis_size(axis)
    other = lax.ppermute(piece, axis, [(i, i ^ (1 << bit)) for i in range(count)])
    return join(piece, other, axis, bit, at)


def join(piece, other, axis, bit, at):
    upper = (lax.axis_index(axis) >> bit) & 1 == 1
    return jnp.where(
        upper, jnp.stack([other, piece], axis=at), jnp.stack([piece, other], axis=at)
    )


def shards(
    flow_state, axial_jacobian, pitch_jacobian, inclination, interface_shift, interface_rows
):
    x = flow_state[0]
    levels, variables, rows, axial = x.shape
    blocks = lax.axis_size("tm")
    slabs = lax.axis_size("pitch")
    row_number = lax.axis_index("row")
    slab = lax.axis_index("pitch")
    slot = (row_number * slabs + slab) % GROUP
    place = jnp.stack([row_number, lax.axis_index("tm"), slab, slot]).astype(jnp.int32)

    time_matrix = jnp.eye(variables, dtype=jnp.float32) - inclination[0] * pitch_jacobian[0]
    matrices = jnp.stack([time_matrix / 12.0, 0.5 * axial_jacobian[0], 0.5 * pitch_jacobian[0]])
    flat = matrices.reshape(-1)
    two = f32(2, variables, rows, axial)
    edge_shape = f32(levels * variables, SUB, LANES)
    piece_size = piece_rows(levels, variables)

    fwd, bwd = pl.pallas_call(
        levels_pack_kernel,
        out_shape=(two, two),
        in_specs=[VM],
        out_specs=(VM, VM),
        compiler_params=params(8),
    )(x)
    edge, piece = pl.pallas_call(
        edge_pack_kernel,
        out_shape=(edge_shape, f32(piece_size, LANES)),
        in_specs=[SM, VM],
        out_specs=(VM, VM),
        compiler_params=params(8),
    )(place, x)
    tables = pl.pallas_call(
        tables_kernel,
        out_shape=f32(1, SUB, LANES),
        in_specs=[SM] + [pl.BlockSpec(memory_space=pltpu.HBM)] * 5,
        out_specs=VM,
        scratch_shapes=[
            pltpu.SMEM((variables, 1, variables), jnp.float32),
            pltpu.SMEM((variables, 1, variables), jnp.float32),
            pltpu.SMEM((1,), jnp.float32),
            pltpu.VMEM((1, rows), jnp.int32),
            pltpu.VMEM((1, rows), jnp.int32),
            pltpu.SemaphoreType.DMA((5,)),
        ],
        compiler_params=params(8),
    )(
        place,
        jnp.transpose(axial_jacobian, (1, 0, 2)),
        jnp.transpose(pitch_jacobian, (1, 0, 2)),
        inclination,
        interface_shift,
        interface_rows,
    )

    def pitch_sides(edge):
        if slabs == 2:
            return lax.ppermute(edge, "pitch", ring(2, 1))
        parts = edge.reshape(levels * variables, 2, 2, 2, LANES)
        below = lax.ppermute(parts[:, :, 0], "pitch", ring(slabs, -1))
        above = lax.ppermute(parts[:, :, 1], "pitch", ring(slabs, 1))
        return jnp.stack([below, above], axis=2).reshape(edge.shape)

    span = slabs * rows
    lanes = 2 * span
    entries = -(-3 * variables * variables // SUB) * SUB
    w_shape = lambda n: (n + 2, variables, levels, blocks, lanes)
    limit = params(10 if blocks * span <= 512 else 60)
    terms = [pltpu.VMEM((WIDTH - 2, variables, levels, blocks, lanes), jnp.float32)] * 2

    side = pitch_sides(edge)
    tbits = (blocks - 1).bit_length()
    ybits = (slabs - 1).bit_length()
    part = piece
    for n in range(tbits - 1):
        part = exchange_bit(part, "tm", tbits - 1 - n, n)

    for k in range(SECTIONS):
        low = lax.ppermute(fwd, "tm", ring(blocks, 1))
        high = lax.ppermute(bwd, "tm", ring(blocks, -1))
        if k == 0:
            bundle = jnp.concatenate([part.reshape(-1, SUB, LANES), tables])
            for n in range(ybits):
                bundle = exchange_bit(bundle, "pitch", ybits - 1 - n, n)
            bundle = exchange_bit(bundle, "row", 0, 0)
            bundle = bundle.reshape((2, slabs) + bundle.shape[-3:])
            tables = bundle[:, :, -1]
            part = bundle[:, :, :-1].reshape(2, slabs, blocks // 2, piece_size, LANES)
            part = exchange_bit(part, "tm", 0, 3)
            part = part.reshape(2, slabs, blocks * piece_size, LANES)
            offsets = tables[:, 0, 0, rows].astype(jnp.int32)
            w0, w1, coef, shift = pl.pallas_call(
                functools.partial(interface_kernel, 0, blocks, slabs, rows, levels, variables),
                out_shape=(
                    f32(*w_shape(WIDTH)),
                    f32(*w_shape(WIDTH - 2)),
                    f32(entries, lanes),
                    f32(blocks, lanes),
                ),
                in_specs=[SM, VM, VM],
                out_specs=(VM,) * 4,
                scratch_shapes=terms,
                compiler_params=limit,
            )(offsets, part, tables)
            strips = pl.pallas_call(
                functools.partial(interface_kernel, 1, blocks, slabs, rows, levels, variables),
                out_shape=f32(levels, variables, rows, LANES),
                in_specs=[SM, SM] + [VM] * 4,
                out_specs=VM,
                scratch_shapes=[
                    pltpu.VMEM(w_shape(WIDTH - 4), jnp.float32),
                    pltpu.VMEM(w_shape(WIDTH - 6), jnp.float32),
                    pltpu.VMEM((SUB, lanes), jnp.float32),
                    *terms,
                ],
                compiler_params=limit,
            )(place, offsets, w0, w1, coef, shift)
        else:
            side = pitch_sides(edge)
        last = k == SECTIONS - 1
        patched = k == SECTIONS - 2
        extra = [strips] if last else []
        inner = pl.pallas_call(
            functools.partial(local_kernel, k, last),
            out_shape=f32(levels, variables, rows, axial),
            in_specs=[SM, SM] + [VM] * (4 + len(extra)),
            out_specs=VM,
            compiler_params=params(8),
        )(flat, place, bwd, fwd, x, side, *extra)
        extra = [strips] if patched else []
        result = pl.pallas_call(
            functools.partial(remote_kernel, k, patched, last),
            out_shape=f32(levels, variables, rows, axial) if last else (two, two, edge_shape),
            in_specs=[SM, SM] + [VM] * (3 + len(extra)),
            out_specs=pl.BlockSpec(memory_space=pltpu.HBM) if last else (VM, VM, VM),
            scratch_shapes=[
                pltpu.VMEM((levels, variables, rows, axial), jnp.float32),
                pltpu.SemaphoreType.DMA((levels,)),
            ]
            if last
            else [],
            compiler_params=params(8),
        )(flat, place, inner, low, high, *extra)
        if not last:
            fwd, bwd, edge = result
    return result[None]


def solution(mesh):
    return jax.shard_map(
        shards,
        mesh=mesh,
        in_specs=(
            P("row", "tm", None, "pitch", None),
            P("row", None, None),
            P("row", None, None),
            P("row"),
            P("row", "pitch"),
            P("row", "pitch"),
        ),
        out_specs=P("row", "tm", None, "pitch", None),
        check_vma=False,
    )
```

```python
import functools

import jax
import jax.numpy as jnp
from jax import lax
from jax.experimental import pallas as pl
from jax.experimental.pallas import tpu as pltpu
from jax.sharding import PartitionSpec as P


SECTIONS = 4
DAMPING = 1.0 / 16.0
LANES = 128
SUB = 8
WIDTH = 12
PATCHED = 6
FLAG = 75
GROUP = 4

VM = pl.BlockSpec(memory_space=pltpu.VMEM)
SM = pl.BlockSpec(memory_space=pltpu.SMEM)


def params(mib):
    return pltpu.CompilerParams(vmem_limit_bytes=mib << 20)


def ring(count, step):
    return [(i, (i + step) % count) for i in range(count)]


def f32(*shape):
    return jax.ShapeDtypeStruct(shape, jnp.float32)


def levels_pack_kernel(x_ref, fwd_ref, bwd_ref):
    levels = x_ref.shape[0]
    fwd_ref[...] = x_ref[levels - 2 :]
    bwd_ref[...] = x_ref[:2]


def piece_rows(levels, variables):
    return -(-(WIDTH // GROUP * levels * variables) // SUB) * SUB


def edge_pack_kernel(place, x_ref, edge_ref, piece_ref):
    levels, variables, rows, axial = x_ref.shape
    rotor = place[0] == 0
    slot = place[3]
    part = lax.broadcasted_iota(jnp.int32, (1, LANES), 1) // rows
    count = piece_ref.shape[0]
    used = WIDTH // GROUP * levels * variables
    piece_ref[used:, :] = jnp.zeros((count - used, LANES), jnp.float32)
    for t in range(levels):
        for v in range(variables):
            for h in range(axial // LANES):
                at = slice(h * LANES, (h + 1) * LANES)
                tile = t * variables + v
                edge_ref[tile, 4 * h : 4 * h + 2] = x_ref[t, v, 0:2, at]
                edge_ref[tile, 4 * h + 2 : 4 * h + 4] = x_ref[t, v, rows - 2 : rows, at]
            tile = jnp.where(rotor, x_ref[t, v, :, axial - LANES :], x_ref[t, v, :, :LANES])
            tile = jnp.transpose(tile)
            tile = jnp.where(rotor, tile[LANES - 2 * SUB :], tile[: 2 * SUB])
            tile = jnp.concatenate([tile] * GROUP, axis=1)
            for hi in range(WIDTH // GROUP):
                total = None
                for lo in range(GROUP):
                    c = hi * GROUP + lo
                    near = jnp.where(
                        rotor, tile[2 * SUB - 1 - c : 2 * SUB - c], tile[c : c + 1]
                    )
                    if total is None:
                        total = near
                    else:
                        total = jnp.where(part == lax.rem(lo + slot, GROUP), near, total)
                row = (hi * variables + v) * levels + t
                piece_ref[row : row + 1, :] = total


def notes_kernel(
    place, axial_ref, pitch_ref, lean_ref, shift_ref, cells_ref, tables, spread
):
    rotor = place[0] == 0
    variables, rows = axial_ref.shape[0], shift_ref.shape[1]
    tables[0] = jnp.zeros((SUB, LANES), jnp.float32)
    tables[0, 0:1, :rows] = shift_ref[...].astype(jnp.float32)
    tables[0, 0:1, rows : 2 * rows] = cells_ref[...].astype(jnp.float32)
    lane = lax.broadcasted_iota(jnp.int32, (1, LANES), 1)
    entries = jnp.zeros((1, LANES), jnp.float32)
    sign = jnp.where(rotor, -1.0, 1.0)
    lean = lean_ref[0, 0]
    for v in range(variables):
        for w in range(variables):
            pitch = pitch_ref[v, 0, w]
            axial = 0.5 * axial_ref[v, 0, w]
            time = ((1.0 if v == w else 0.0) - lean * pitch) * (1.0 / 12.0)
            for m, (value, shared) in enumerate(
                ((time, time), (axial, sign * axial), (0.5 * pitch, 0.5 * pitch))
            ):
                at = (m * variables + v) * variables + w
                spread[at : at + 1, :] = jnp.full((1, LANES), value)
                entries = jnp.where(lane == at, shared, entries)
    tables[0, 1:2, :] = entries
    spread[FLAG : FLAG + 1, :] = jnp.full((1, LANES), jnp.where(rotor, 1.0, 0.0))


def local_kernel(section, has_pad, *refs):
    coef, bwd, fwd, init, edge = refs[:5]
    pad = refs[5] if has_pad else None
    rotor = jnp.broadcast_to(coef[FLAG : FLAG + 1, :], (SUB, LANES)) > 0.5
    out = refs[-1]
    levels, variables, rows, axial = init.shape
    tiles, groups = axial // LANES, rows // SUB
    factor = 1.0 / (SECTIONS - section)
    lane = lax.broadcasted_iota(jnp.int32, (SUB, LANES), 1)
    sub = lax.broadcasted_iota(jnp.int32, (SUB, LANES), 0)

    def cell(t, v, g, h):
        ref, index = (bwd, t) if t < 2 else (fwd, t - (levels - 2))
        return ref[index, v, SUB * g : SUB * g + SUB, h * LANES : (h + 1) * LANES]

    for g in range(groups):
        for h in range(tiles):
            center = {}
            for t in range(levels):
                for v in range(variables):
                    center[t, v] = cell(t, v, g, h)
            for t in range(levels):
                rates = []
                smooth = []
                for v in range(variables):
                    c = center[t, v]
                    if g == 0:
                        above = pltpu.roll(edge[t * variables + v], (4 - 4 * h) % SUB, 0)
                    else:
                        above = cell(t, v, g - 1, h)
                    if g == groups - 1:
                        below = pltpu.roll(edge[t * variables + v], (SUB - 4 * h) % SUB, 0)
                    else:
                        below = cell(t, v, g + 1, h)
                    j_m1 = pltpu.roll(jnp.where(sub >= 7, above, c), 1, 0)
                    j_m2 = pltpu.roll(jnp.where(sub >= 6, above, c), 2, 0)
                    j_p1 = pltpu.roll(jnp.where(sub < 1, below, c), 7, 0)
                    j_p2 = pltpu.roll(jnp.where(sub < 2, below, c), 6, 0)
                    zero = jnp.zeros_like(c)
                    beyond = pad[t, v, SUB * g : SUB * g + SUB] if has_pad else zero
                    if h > 0:
                        left = cell(t, v, g, h - 1)
                    else:
                        left = jnp.where(rotor, zero, beyond) if has_pad else zero
                    if h < tiles - 1:
                        right = cell(t, v, g, h + 1)
                    else:
                        right = jnp.where(rotor, beyond, zero) if has_pad else zero
                    a_m1 = pltpu.roll(jnp.where(lane >= LANES - 1, left, c), 1, 1)
                    a_m2 = pltpu.roll(jnp.where(lane >= LANES - 2, left, c), 2, 1)
                    a_p1 = pltpu.roll(jnp.where(lane < 1, right, c), LANES - 1, 1)
                    a_p2 = pltpu.roll(jnp.where(lane < 2, right, c), LANES - 2, 1)
                    near = (j_m1 + j_p1) + (a_m1 + a_p1)
                    far = (j_m2 + j_p2) + (a_m2 + a_p2)
                    rate = None
                    for step, weight in ((-2, 1.0), (-1, -8.0), (1, 8.0), (2, -1.0)):
                        if 0 <= t + step < levels:
                            u = center[t + step, v]
                            if abs(step) == 1:
                                near = near + u
                                u = weight * u
                                rate = u if rate is None else rate + u
                            else:
                                far = far + u
                                if rate is None:
                                    rate = weight * u
                                else:
                                    rate = rate + u if weight > 0 else rate - u
                    smooth.append(18.0 * c - 4.0 * near + far)
                    rates.append((rate, a_p1 - a_m1, j_p1 - j_m1))
                for v in range(variables):
                    total = smooth[v] * DAMPING
                    for w in range(variables):
                        for m in range(3):
                            entry = (m * variables + v) * variables + w
                            total = total + coef[entry : entry + 1, :] * rates[w][m]
                    at = (t, v, slice(SUB * g, SUB * g + SUB), slice(h * LANES, (h + 1) * LANES))
                    out[at] = init[at] - factor * total


def remote_kernel(section, patched, last, *refs):
    coef, part, low, high = refs[:4]
    patch = refs[4] if patched else None
    outs = refs[5:] if patched else refs[4:]
    levels, variables, rows, axial = part.shape
    if last:
        result, built, sems = outs
        outs = (built,)
    tiles, groups = axial // LANES, rows // SUB
    factor = 1.0 / (SECTIONS - section)
    if patched:
        lane = lax.broadcasted_iota(jnp.int32, (SUB, LANES), 1)
        rotor = jnp.broadcast_to(coef[FLAG : FLAG + 1, :], (SUB, LANES)) > 0.5

    def block(g, h, wanted):
        js = slice(SUB * g, SUB * g + SUB)
        at = slice(h * LANES, (h + 1) * LANES)

        def level(t, v):
            if t < 0:
                return low[t + 2, v, js, at]
            return high[t - levels, v, js, at]

        for t in wanted:
            rates = []
            smooth = []
            for v in range(variables):
                rate = None
                near = None
                far = None
                for step, weight in ((-2, 1.0), (-1, -8.0), (1, 8.0), (2, -1.0)):
                    if not 0 <= t + step < levels:
                        u = level(t + step, v)
                        if abs(step) == 1:
                            near = u if near is None else near + u
                        else:
                            far = u if far is None else far + u
                        u = u if weight == 1.0 else weight * u
                        rate = u if rate is None else rate + u
                q = None
                if near is not None:
                    q = -4.0 * near
                if far is not None:
                    q = far if q is None else q + far
                rates.append(rate)
                smooth.append(q)
            for v in range(variables):
                total = smooth[v] * DAMPING
                for w in range(variables):
                    at_row = v * variables + w
                    total = total + coef[at_row : at_row + 1, :] * rates[w]
                new = part[t, v, js, at] - factor * total
                if patched:
                    if h == 0:
                        new = jnp.where((lane < PATCHED) & ~rotor, patch[t, v, js], new)
                    if h == tiles - 1:
                        new = jnp.where(
                            (lane >= LANES - PATCHED) & rotor, patch[t, v, js], new
                        )
                if last:
                    outs[0][t, v, js, at] = new
                    continue
                fwd, bwd, edge = outs
                if t < 2:
                    bwd[t, v, js, at] = new
                if t >= levels - 2:
                    fwd[t - (levels - 2), v, js, at] = new
                if g == 0:
                    edge[t * variables + v, 4 * h : 4 * h + 2] = new[0:2]
                if g == groups - 1:
                    edge[t * variables + v, 4 * h + 2 : 4 * h + 4] = new[6:8]

    if not last:
        for g in range(groups):
            for h in range(tiles):
                block(g, h, range(levels))
        return
    copies = []
    for t in range(levels):
        for g in range(groups):
            for h in range(tiles):
                block(g, h, (t,))
        for v in range(variables):
            at = t * variables + v
            copies.append(pltpu.make_async_copy(built.at[t, v], result.at[t, v], sems.at[at]))
            copies[-1].start()
    for copy in copies:
        copy.wait()


def unpack_interface(blocks, slabs, rows, levels, variables, part, refs):
    _, gathered, tables, w0, _, coef, shift_ref, _, _ = refs
    span = slabs * rows
    lanes = 2 * span
    count = piece_rows(levels, variables)

    for hi in range(WIDTH // GROUP):
        for v in range(variables):
            for d in range(levels):
                row = (hi * variables + v) * levels + d
                for tile in range(lanes // LANES):
                    got = []
                    for n in range(GROUP):
                        x, y = divmod(GROUP * tile + n, slabs)
                        got.append(gathered[x, y, pl.ds(row, blocks, stride=count), :])
                    for lo in range(GROUP):
                        total = got[0]
                        for n in range(1, GROUP):
                            total = jnp.where(part == (lo + n) % GROUP, got[n], total)
                        if lo:
                            total = pltpu.roll(total, LANES - rows * lo, 1)
                        at = slice(tile * LANES, (tile + 1) * LANES)
                        w0[hi * GROUP + lo + 2, v, d, :, at] = total

    sides = []
    for x in range(2):
        turned = jnp.transpose(tables[x, 0])[:, 1:2]
        sides.append(jnp.broadcast_to(turned, (LANES, LANES)))
    lower = lax.broadcasted_iota(jnp.int32, (LANES, LANES), 1) >= span
    for tile in range(lanes // LANES):
        at = slice(tile * LANES, (tile + 1) * LANES)
        if lanes == LANES:
            both = jnp.where(lower, sides[1], sides[0])
        else:
            both = sides[(tile * LANES) // span]
        coef[:, at] = both[: coef.shape[0]]

    for tile in range(lanes // LANES):
        total = None
        for n in range(GROUP):
            x, y = divmod(GROUP * tile + n, slabs)
            table = tables[x, y, 0:1, :]
            moved = jnp.broadcast_to(pltpu.roll(table, rows * n, 1) if n else table, (blocks, LANES))
            total = moved if total is None else jnp.where(part == n, moved, total)
        shift_ref[:, tile * LANES : (tile + 1) * LANES] = total


def interface_kernel(half, blocks, slabs, rows, levels, variables, *refs):
    if half == 0:
        offsets, _, _, w0, w1, coef, shift_ref, smooth_terms, rate_terms = refs
    else:
        place, offsets, w0, w1, coef, shift_ref, strips, w2, w3, strip, smooth_terms, rate_terms = refs
    span = slabs * rows
    lanes = 2 * span
    lane = lax.broadcasted_iota(jnp.int32, (blocks, lanes), 1)
    second = lane >= span
    part = lax.broadcasted_iota(jnp.int32, (blocks, LANES), 1) // rows
    if half == 0:
        unpack_interface(blocks, slabs, rows, levels, variables, part, refs)
    shift = shift_ref[...].astype(jnp.int32)
    coarse = shift // levels
    fine = shift - levels * coarse

    source = lax.broadcasted_iota(jnp.int32, (lanes, lanes), 0)
    target = lax.broadcasted_iota(jnp.int32, (lanes, lanes), 1)
    base = jnp.where(target >= span, span, 0)
    cell = target - base

    def picks(s):
        return (source == base + lax.rem(cell + (span + s), span)).astype(jnp.float32)

    one_away = picks(-1), picks(1)
    smoothing = (picks(-2) + picks(2)) - 4.0 * (one_away[0] + one_away[1])
    pitch_terms = jnp.concatenate([smoothing, one_away[1] - one_away[0]], axis=1)
    read = lax.rem(cell + jnp.where(target >= span, offsets[1], offsets[0]), span)
    remap = (source == (span - base) + read).astype(jnp.float32)

    def for_parts(matrix):
        return jnp.concatenate([matrix.astype(jnp.bfloat16)] * 3, axis=0)

    pitch_terms, remap = for_parts(pitch_terms), for_parts(remap)

    def product(u, matrix):
        high = u.astype(jnp.bfloat16)
        rest = u - high.astype(jnp.float32)
        middle = rest.astype(jnp.bfloat16)
        low = (rest - middle.astype(jnp.float32)).astype(jnp.bfloat16)
        parts = jnp.concatenate([high, middle, low], axis=1)
        return jnp.dot(parts, matrix, preferred_element_type=jnp.float32)

    pair_shape = (2, variables, levels, blocks, lanes)

    def flat(w, c):
        return w[c : c + 2].reshape(-1, lanes)

    def later(w, c, v, d):
        if d >= levels:
            return pltpu.roll(w[c, v, d - levels], blocks - 1, 0)
        if d < 0:
            return pltpu.roll(w[c, v, d + levels], 1, 0)
        return w[c, v, d]

    def fill_ghosts(w):
        moved_cells = product(flat(w, 2), remap).reshape(pair_shape)
        for c in range(2):
            for v in range(variables):
                seen = [moved_cells[c, v, d] for d in range(levels)]
                wrapped = [pltpu.roll(seen[d], blocks - 1, 0) for d in range(levels - 1)]
                for d in range(levels):
                    value = seen[d]
                    for f in range(1, levels):
                        moved = seen[d + f] if d + f < levels else wrapped[d + f - levels]
                        value = jnp.where(fine == f, moved, value)
                    for bit in range((blocks - 1).bit_length()):
                        moved = pltpu.roll(value, blocks - (1 << bit), 0)
                        value = jnp.where((coarse >> bit) & 1 == 1, moved, value)
                    w[1 - c, v, d] = value

    def across(w, cells):
        for c in range(0, cells, 2):
            terms = product(flat(w, c + 2), pitch_terms)
            smooth_terms[c : c + 2] = terms[:, :lanes].reshape(pair_shape)
            rate_terms[c : c + 2] = terms[:, lanes:].reshape(pair_shape)

    def advance(w, new, cells, section):
        factor = 1.0 / (SECTIONS - section)

        def one(c, carry):
            for d in range(levels):
                rates = []
                smooth = []
                for v in range(variables):
                    u = w[c, v, d]
                    m2, m1, p1, p2 = (later(w, c, v, d + s) for s in (-2, -1, 1, 2))
                    l2, l1 = w[c - 2, v, d], w[c - 1, v, d]
                    r1, r2 = w[c + 1, v, d], w[c + 2, v, d]
                    near = (m1 + p1) + (l1 + r1)
                    far = (m2 + p2) + (l2 + r2)
                    smooth.append((18.0 * u - 4.0 * near) + (far + smooth_terms[c - 2, v, d]))
                    rates.append(((m2 - p2) + 8.0 * (p1 - m1), r1 - l1, rate_terms[c - 2, v, d]))
                for v in range(variables):
                    total = smooth[v] * DAMPING
                    for m in range(3):
                        for k in range(variables):
                            at = (m * variables + v) * variables + k
                            total = total + coef[at : at + 1, :] * rates[k][m]
                    new[c, v, d] = w0[c, v, d] - factor * total
            return carry

        across(w, cells)
        lax.fori_loop(2, 2 + cells, one, 0)

    if half == 0:
        fill_ghosts(w0)
        advance(w0, w1, WIDTH - 2, 0)
        fill_ghosts(w1)
        return
    advance(w1, w2, WIDTH - 4, 1)
    fill_ghosts(w2)
    advance(w2, w3, WIDTH - 6, 2)
    fill_ghosts(w3)

    row, block, slab = place[0], place[1], place[2]
    rotor = row == 0
    start = row * span + slab * rows
    first_lane = jnp.where(rotor, LANES - PATCHED, LANES - 2)
    for d in range(levels):
        for v in range(variables):
            for q in range(SUB):
                c = jnp.where(rotor, SUB - 1 - q, q)
                strip[q : q + 1, :] = w3[c, v, d, pl.ds(block, 1), :]
            own = pltpu.roll(strip[...], lanes - start, 1)[:, :LANES]
            turned = jnp.transpose(own)[:rows, :]
            wide = jnp.concatenate(
                [turned, jnp.zeros((rows, LANES - SUB), jnp.float32)], axis=1
            )
            strips[d, v] = pltpu.roll(wide, first_lane, 1)


def exchange_bit(piece, axis, bit, at):
    count = lax.axis_size(axis)
    other = lax.ppermute(piece, axis, [(i, i ^ (1 << bit)) for i in range(count)])
    return join(piece, other, axis, bit, at)


def join(piece, other, axis, bit, at):
    upper = (lax.axis_index(axis) >> bit) & 1 == 1
    return jnp.where(
        upper, jnp.stack([other, piece], axis=at), jnp.stack([piece, other], axis=at)
    )


def shards(
    flow_state, axial_jacobian, pitch_jacobian, inclination, interface_shift, interface_rows
):
    x = flow_state[0]
    levels, variables, rows, axial = x.shape
    blocks = lax.axis_size("tm")
    slabs = lax.axis_size("pitch")
    row_number = lax.axis_index("row")
    slab = lax.axis_index("pitch")
    slot = (row_number * slabs + slab) % GROUP
    place = jnp.stack([row_number, lax.axis_index("tm"), slab, slot]).astype(jnp.int32)

    two = f32(2, variables, rows, axial)
    edge_shape = f32(levels * variables, SUB, LANES)
    piece_size = piece_rows(levels, variables)

    fwd, bwd = pl.pallas_call(
        levels_pack_kernel,
        out_shape=(two, two),
        in_specs=[VM],
        out_specs=(VM, VM),
        compiler_params=params(8),
    )(x)
    edge, piece = pl.pallas_call(
        edge_pack_kernel,
        out_shape=(edge_shape, f32(piece_size, LANES)),
        in_specs=[SM, VM],
        out_specs=(VM, VM),
        compiler_params=params(8),
    )(place, x)
    tables, spread = pl.pallas_call(
        notes_kernel,
        out_shape=(
            f32(1, SUB, LANES),
            f32(-(-(FLAG + 1) // SUB) * SUB, LANES),
        ),
        in_specs=[SM] * 4 + [VM] * 2,
        out_specs=(VM, VM),
        compiler_params=params(8),
    )(
        place,
        jnp.transpose(axial_jacobian, (1, 0, 2)),
        jnp.transpose(pitch_jacobian, (1, 0, 2)),
        inclination.reshape(1, 1),
        interface_shift,
        interface_rows,
    )

    def pitch_sides(edge):
        if slabs == 2:
            return lax.ppermute(edge, "pitch", ring(2, 1))
        parts = edge.reshape(levels * variables, 2, 2, 2, LANES)
        below = lax.ppermute(parts[:, :, 0], "pitch", ring(slabs, -1))
        above = lax.ppermute(parts[:, :, 1], "pitch", ring(slabs, 1))
        return jnp.stack([below, above], axis=2).reshape(edge.shape)

    span = slabs * rows
    lanes = 2 * span
    entries = -(-3 * variables * variables // SUB) * SUB
    w_shape = lambda n: (n + 2, variables, levels, blocks, lanes)
    limit = params(10 if blocks * span <= 512 else 60)
    terms = [pltpu.VMEM((WIDTH - 2, variables, levels, blocks, lanes), jnp.float32)] * 2

    side = pitch_sides(edge)
    tbits = (blocks - 1).bit_length()
    ybits = (slabs - 1).bit_length()
    part = piece
    for n in range(tbits - 1):
        part = exchange_bit(part, "tm", tbits - 1 - n, n)

    for k in range(SECTIONS):
        low = lax.ppermute(fwd, "tm", ring(blocks, 1))
        high = lax.ppermute(bwd, "tm", ring(blocks, -1))
        if k == 0:
            bundle = jnp.concatenate([part.reshape(-1, SUB, LANES), tables])
            for n in range(ybits):
                bundle = exchange_bit(bundle, "pitch", ybits - 1 - n, n)
            bundle = exchange_bit(bundle, "row", 0, 0)
            bundle = bundle.reshape((2, slabs) + bundle.shape[-3:])
            tables = bundle[:, :, -1]
            part = bundle[:, :, :-1].reshape(2, slabs, blocks // 2, piece_size, LANES)
            part = exchange_bit(part, "tm", 0, 3)
            part = part.reshape(2, slabs, blocks * piece_size, LANES)
            offsets = tables[:, 0, 0, rows].astype(jnp.int32)
            w0, w1, coef, shift = pl.pallas_call(
                functools.partial(interface_kernel, 0, blocks, slabs, rows, levels, variables),
                out_shape=(
                    f32(*w_shape(WIDTH)),
                    f32(*w_shape(WIDTH - 2)),
                    f32(entries, lanes),
                    f32(blocks, lanes),
                ),
                in_specs=[SM, VM, VM],
                out_specs=(VM,) * 4,
                scratch_shapes=terms,
                compiler_params=limit,
            )(offsets, part, tables)
            strips = pl.pallas_call(
                functools.partial(interface_kernel, 1, blocks, slabs, rows, levels, variables),
                out_shape=f32(levels, variables, rows, LANES),
                in_specs=[SM, SM] + [VM] * 4,
                out_specs=VM,
                scratch_shapes=[
                    pltpu.VMEM(w_shape(WIDTH - 4), jnp.float32),
                    pltpu.VMEM(w_shape(WIDTH - 6), jnp.float32),
                    pltpu.VMEM((SUB, lanes), jnp.float32),
                    *terms,
                ],
                compiler_params=limit,
            )(place, offsets, w0, w1, coef, shift)
        else:
            side = pitch_sides(edge)
        last = k == SECTIONS - 1
        patched = k == SECTIONS - 2
        extra = [strips] if last else []
        inner = pl.pallas_call(
            functools.partial(local_kernel, k, last),
            out_shape=f32(levels, variables, rows, axial),
            in_specs=[VM] * (5 + len(extra)),
            out_specs=VM,
            compiler_params=params(8),
        )(spread, bwd, fwd, x, side, *extra)
        extra = [strips] if patched else []
        result = pl.pallas_call(
            functools.partial(remote_kernel, k, patched, last),
            out_shape=f32(levels, variables, rows, axial) if last else (two, two, edge_shape),
            in_specs=[VM] * (4 + len(extra)),
            out_specs=pl.BlockSpec(memory_space=pltpu.HBM) if last else (VM, VM, VM),
            scratch_shapes=[
                pltpu.VMEM((levels, variables, rows, axial), jnp.float32),
                pltpu.SemaphoreType.DMA((levels * variables,)),
            ]
            if last
            else [],
            compiler_params=params(8),
        )(spread, inner, low, high, *extra)
        if not last:
            fwd, bwd, edge = result
    return result[None]


def solution(mesh):
    return jax.shard_map(
        shards,
        mesh=mesh,
        in_specs=(
            P("row", "tm", None, "pitch", None),
            P("row", None, None),
            P("row", None, None),
            P("row"),
            P("row", "pitch"),
            P("row", "pitch"),
        ),
        out_specs=P("row", "tm", None, "pitch", None),
        check_vma=False,
    )
```
